32 devices in a mesh: row: 4 (over x, core), col: 8 (over z, y).
Axes of the slice: x: 2, y: 2, z: 4, core: 2. Of those that a mesh axis runs over, the one named last changes fastest.
Arguments:
- object_field: float32 [2, 1024, 2048], P(None, 'row', 'col'), may hold values from -6 to 6
- probe: float32 [2, 128, 128], replicated, may hold values from -6 to 6
- amplitude: bfloat16 [4, 8, 16, 128, 128], P('row', 'col'), may hold values from 0 to 2
- corners: int32 [2, 4, 8, 16], P(None, 'row', 'col'), may hold values from 0 to 255, as said below
- live_count: int32 [4, 8], P('row', 'col'), may hold values from 4 to 16, as said below
Outputs:
- refined_object: float32 [2, 1024, 2048], P(None, 'row', 'col')
- new_probe: float32 [2, 128, 128], replicated
The draws below stay inside these ranges and needn't reach their ends.
Inputs may be any that keep to these rules, and one draw needn't show every extreme that they name: In the last tile row of the mesh corners[0] is at most 128, and in the last tile column corners[1] is at most 128, so every window lies inside the object. Outside the last tile row, corners[0] of slot 0 is at least 192; outside the last tile column, corners[1] of slot 0 is at least 192. Unused slots carry valid corners. Slots from live_count on are unused. Some tile uses all 16 slots in every draw.
All inputs are finite; a program needn't handle non-finite values.
Results may differ from the reference program's by a relative error of at most 0.0039.
The reference program's roundings to bfloat16 on the way count: a program that leaves them out, or rounds other values in their place, can miss the bound.
Values may be sent and summed in bfloat16 or wider, within the bound.
A program may use at most 64 MiB of HBM per device.

```python
import math
import jax
import jax.numpy as jnp
from jax import lax

WIN = 128
TILE = 256
SLOTS = 16
BLOCK = 4
NR = 1024
NC = 2048
N_ROW = 4
N_COL = 8


def draw_corners(key, part):
    base_key = jax.random.fold_in(key, 11)
    first_key = jax.random.fold_in(base_key, 1)
    second_key = jax.random.fold_in(base_key, 2)
    third_key = jax.random.fold_in(base_key, 3)
    fourth_key = jax.random.fold_in(base_key, 4)
    field_shape = (N_ROW, N_COL, SLOTS)
    tile_rows = jnp.broadcast_to(jnp.arange(N_ROW, dtype=jnp.int32)[:, None, None], field_shape)
    tile_cols = jnp.broadcast_to(jnp.arange(N_COL, dtype=jnp.int32)[None, :, None], field_shape)
    slot_number = jnp.broadcast_to(jnp.arange(SLOTS, dtype=jnp.int32)[None, None, :], field_shape)
    row_limit = jnp.where(tile_rows == N_ROW - 1, TILE - WIN + 1, TILE)
    col_limit = jnp.where(tile_cols == N_COL - 1, TILE - WIN + 1, TILE)
    row_pick = jax.random.randint(first_key, field_shape, 0, row_limit)
    col_pick = jax.random.randint(second_key, field_shape, 0, col_limit)
    row_edge = TILE - WIN // 2 + jax.random.randint(third_key, field_shape, 0, WIN // 2)
    col_edge = TILE - WIN // 2 + jax.random.randint(fourth_key, field_shape, 0, WIN // 2)
    row_pick = jnp.where((slot_number == 0) & (tile_rows < N_ROW - 1), row_edge, row_pick)
    col_pick = jnp.where((slot_number == 0) & (tile_cols < N_COL - 1), col_edge, col_pick)
    return jnp.stack([row_pick, col_pick]).astype(jnp.int32)


def draw_live_count(key, part):
    base_key = jax.random.fold_in(key, 23)
    first_key = jax.random.fold_in(base_key, 1)
    second_key = jax.random.fold_in(base_key, 2)
    divisor = 1 + jax.random.randint(first_key, (N_ROW * N_COL,), 0, 4)
    counted = SLOTS // divisor
    chosen = jax.random.randint(second_key, (), 0, N_ROW * N_COL)
    counted = jnp.where(jnp.arange(N_ROW * N_COL) == chosen, SLOTS, counted)
    return counted.reshape(N_ROW, N_COL).astype(jnp.int32)


def block_levels(rng, shape, shards, least, high):
    def one(position, parts):
        draws = jax.random.uniform(jax.random.fold_in(jax.random.fold_in(rng, 6), position), (parts,), jnp.float32, least / len(shards), high / len(shards))
        return jnp.repeat(jnp.exp(draws), shape[position] // parts).reshape((-1,) + (1,) * (len(shape) - position - 1))

    loudness = one(*shards[0])
    for cut in shards[1:]:
        loudness = loudness * one(*cut)
    return loudness


def gaussian(rng, dims, scale, most, split=(), held_as=jnp.bfloat16):
    drawn = jax.random.normal(rng, dims, jnp.float32) * scale
    if len(split) > 0:
        drawn = block_levels(rng, dims, split, -0.22, 0.18) * drawn
    return jnp.clip(drawn, min=-most, max=most).astype(held_as)


def setup_inputs(seed: int = 0) -> dict:
    arg_keys = jax.random.split(jax.random.key(seed), 6)
    object_field = gaussian(arg_keys[0], (2, NR, NC), 1.0, 6.0, ((1, 4), (2, 8)), jnp.float32)
    probe = gaussian(arg_keys[1], (2, WIN, WIN), 1.0, 6.0, (), jnp.float32)
    amplitude = jnp.clip(2.0 * jax.random.uniform(arg_keys[2], (N_ROW, N_COL, SLOTS, WIN, WIN), jnp.float32) ** block_levels(arg_keys[2], (N_ROW, N_COL, SLOTS, WIN, WIN), ((0, 4), (1, 8)), -0.2, 0.2), 0.0, 2.0).astype(jnp.bfloat16)
    corners = draw_corners(jax.random.fold_in(arg_keys[5], 71), 0)
    live_count = draw_live_count(jax.random.fold_in(arg_keys[5], 71), 0)
    return {"object_field": object_field, "probe": probe, "amplitude": amplitude, "corners": corners, "live_count": live_count}


def dft_tables(window):
    indices = jnp.arange(window, dtype=jnp.int32)
    phase_index = indices[:, None] * indices[None, :] % window
    angles = phase_index.astype(jnp.float32) * (2.0 * math.pi / window)
    norming = 1.0 / math.sqrt(window)
    cosines = jnp.cos(angles) * norming
    sines = jnp.sin(angles) * norming
    forward_fourier = jnp.stack([jnp.stack([cosines, -sines]), jnp.stack([sines, cosines])])
    inverse_fourier = jnp.stack([jnp.stack([cosines, sines]), jnp.stack([-sines, cosines])])
    return (forward_fourier.astype(jnp.bfloat16), inverse_fourier.astype(jnp.bfloat16))

def times(left_value, right_value):
    real_part = left_value[..., 0, :, :] * right_value[..., 0, :, :] - left_value[..., 1, :, :] * right_value[..., 1, :, :]
    imag_part = left_value[..., 0, :, :] * right_value[..., 1, :, :] + left_value[..., 1, :, :] * right_value[..., 0, :, :]
    return jnp.stack([real_part, imag_part], -3)

def times_conj(left_value, right_value):
    real_part = left_value[..., 0, :, :] * right_value[..., 0, :, :] + left_value[..., 1, :, :] * right_value[..., 1, :, :]
    imag_part = left_value[..., 0, :, :] * right_value[..., 1, :, :] - left_value[..., 1, :, :] * right_value[..., 0, :, :]
    return jnp.stack([real_part, imag_part], -3)

def refine_object(exit_waves, measured_intensity, forward_fourier, inverse_fourier):
    highest = lax.Precision.HIGHEST
    forward_wide = forward_fourier.astype(jnp.float32)
    inverse_wide = inverse_fourier.astype(jnp.float32)
    half_done = jnp.einsum('bcrk,cdkm->bdrm', exit_waves.astype(jnp.float32), forward_wide, precision=highest).astype(jnp.bfloat16)
    spectrum = jnp.einsum('cdrs,bcsm->bdrm', forward_wide, half_done.astype(jnp.float32), precision=highest)
    modulus = jnp.sqrt(spectrum[:, 0] * spectrum[:, 0] + spectrum[:, 1] * spectrum[:, 1])
    rescale = measured_intensity.astype(jnp.float32) / jnp.maximum(modulus, 0.5)
    projected = (spectrum * rescale[:, None]).astype(jnp.bfloat16)
    half_back = jnp.einsum('bcrk,cdkm->bdrm', projected.astype(jnp.float32), inverse_wide, precision=highest).astype(jnp.bfloat16)
    returned = jnp.einsum('cdrs,bcsm->bdrm', inverse_wide, half_back.astype(jnp.float32), precision=highest)
    return returned - exit_waves.astype(jnp.float32)

def reference(object_field, probe, amplitude, corners, live_count):
    forward_fourier, inverse_fourier = dft_tables(WIN)
    tile_rows = jnp.arange(N_ROW, dtype=jnp.int32)[:, None, None] * TILE
    tile_cols = jnp.arange(N_COL, dtype=jnp.int32)[None, :, None] * TILE
    row_start = (corners[0].astype(jnp.int32) + tile_rows).reshape(-1, BLOCK)
    col_start = (corners[1].astype(jnp.int32) + tile_cols).reshape(-1, BLOCK)
    used = (jnp.arange(SLOTS, dtype=jnp.int32)[None, None, :] < live_count[:, :, None]).reshape(-1, BLOCK)
    measured_all = amplitude.reshape(-1, BLOCK, WIN, WIN)
    power = probe[0] * probe[0] + probe[1] * probe[1]
    zero_index = jnp.zeros((), jnp.int32)

    def sweep(current):

        def advance(carry, item):
            summed, lighting, gradient = carry
            starts_r, starts_c, update_marks, measured_intensity = item
            patches = jax.vmap(lambda row_at, col_at: lax.dynamic_slice(current, (zero_index, row_at, col_at), (2, WIN, WIN)))(starts_r, starts_c)
            exit_waves = times(probe[None], patches).astype(jnp.bfloat16)
            weights = update_marks.astype(jnp.float32)
            object_delta = lax.cond(jnp.any(update_marks), lambda exit_wave_portion, measurement_portion: refine_object(exit_wave_portion, measurement_portion, forward_fourier, inverse_fourier), lambda exit_wave_portion, measurement_portion: jnp.zeros(exit_wave_portion.shape, jnp.float32), exit_waves, measured_intensity)
            object_delta = object_delta * weights[:, None, None, None]
            pushed = times_conj(probe[None], object_delta)
            for member in range(BLOCK):
                anchor = (zero_index, starts_r[member], starts_c[member])
                summed = lax.dynamic_update_slice(summed, lax.dynamic_slice(summed, anchor, (2, WIN, WIN)) + pushed[member], anchor)
                flat_anchor = (starts_r[member], starts_c[member])
                lighting = lax.dynamic_update_slice(lighting, lax.dynamic_slice(lighting, flat_anchor, (WIN, WIN)) + power * weights[member], flat_anchor)
            gradient = gradient + lax.optimization_barrier(jnp.sum(times_conj(patches, object_delta), 0))
            return ((summed, lighting, gradient), None)
        start_carry = (jnp.zeros((2, NR, NC), jnp.float32), jnp.zeros((NR, NC), jnp.float32), jnp.zeros((2, WIN, WIN), jnp.float32))
        final_carry, ignored = lax.scan(advance, start_carry, (row_start, col_start, used, measured_all))
        return final_carry
    summed, lighting, first_grad = sweep(object_field)
    denominator = lighting + 4.0
    updated = object_field + summed / denominator
    summed_two, second_light, gradient = sweep(updated)
    refined_object = updated + summed_two / denominator
    spread = jnp.sqrt(jnp.mean(gradient[0] * gradient[0] + gradient[1] * gradient[1]) + 1e-06)
    new_probe = probe + gradient / spread
    return (refined_object, new_probe)
```

```python
import functools
import math

import jax
import jax.numpy as jnp
import numpy as np
from jax import lax
from jax.experimental import pallas as pl
from jax.experimental.pallas import tpu as pltpu
from jax.sharding import PartitionSpec as P

GROUP = 4


def from_behind(value, axis, steps):
    count = lax.axis_size(axis)
    first, last = (max(0, -steps), min(count, count - steps))
    return lax.ppermute(value, axis, [(source, source + steps) for source in range(first, last)])


def dft_tables(window):
    indices = np.arange(window, dtype=np.int32)
    phase_index = indices[:, None] * indices[None, :] % window
    angles = phase_index.astype(np.float32) * np.float32(2.0 * math.pi / window)
    norming = np.float32(1.0 / math.sqrt(window))
    cosines = np.cos(angles) * norming
    sines = np.sin(angles) * norming
    forward = np.block([[cosines, -sines], [sines, cosines]]).astype(np.float32)
    return (jnp.asarray(forward, jnp.bfloat16), jnp.asarray(forward.T.copy(), jnp.bfloat16))


def dot(left, right):
    return jnp.dot(left, right, preferred_element_type=jnp.float32)


def sweep_kernel(with_light, corners, live, ext, probe, amp, ahead, back, deposit, *rest):
    if with_light:
        waves_buf = rest[0]
    else:
        gradient, waves_buf, patch_buf = rest
        gradient[...] = jnp.zeros_like(gradient)
    slots, win = amp.shape[0], amp.shape[1]
    deposit[...] = jnp.zeros_like(deposit)
    lane = lax.broadcasted_iota(jnp.int32, (win, win), 1)
    used = live[0]

    def spot(slot):
        row, col = corners[0, slot], corners[1, slot]
        base = col // win
        return row, base, col - base * win

    def add_at(plane, row, base, shift, value):
        turned = pltpu.roll(value, shift, 1)
        left = jnp.where(lane >= shift, turned, 0.0)
        right = jnp.where(lane >= shift, 0.0, turned)
        for offset, part in ((0, left), (1, right)):
            at = (plane, base + offset, pl.ds(row, win))
            deposit[at] = deposit[at] + part

    @pl.loop(0, (used + GROUP - 1) // GROUP)
    def _(turn):
        first = turn * GROUP
        pr, pi = probe[0], probe[1]
        for member in range(GROUP):
            row, base, shift = spot(first + member)
            parts = []
            for plane in range(2):
                left = ext[plane, base, pl.ds(row, win)]
                right = ext[plane, base + 1, pl.ds(row, win)]
                mixed = jnp.where(lane >= shift, left, right)
                parts.append(pltpu.roll(mixed, lax.rem(win - shift, win), 1))
            re, im = parts
            if not with_light:
                patch_buf[member, 0] = re
                patch_buf[member, 1] = im
            rows = pl.ds(member * win, win)
            waves_buf[rows, :win] = (pr * re - pi * im).astype(jnp.bfloat16)
            waves_buf[rows, win:] = (pr * im + pi * re).astype(jnp.bfloat16)
        half = dot(waves_buf[...], ahead[...]).astype(jnp.bfloat16)

        def upright(value):
            columns = []
            for member in range(GROUP):
                block = value[member * win : (member + 1) * win]
                columns.append(jnp.concatenate([block[:, :win], block[:, win:]], 0))
            return jnp.concatenate(columns, 1)

        spectrum = dot(back[...], upright(half))
        projected = []
        for member in range(GROUP):
            re = spectrum[:win, member * win : (member + 1) * win]
            im = spectrum[win:, member * win : (member + 1) * win]
            scale = amp[first + member].astype(jnp.float32) * lax.rsqrt(
                jnp.maximum(re * re + im * im, 0.25)
            )
            projected.append(
                jnp.concatenate(
                    [(re * scale).astype(jnp.bfloat16), (im * scale).astype(jnp.bfloat16)], 1
                )
            )
        half_back = dot(jnp.concatenate(projected, 0), back[...]).astype(jnp.bfloat16)
        returned = dot(ahead[...], upright(half_back))
        for member in range(GROUP):
            slot = first + member
            weight = jnp.where(slot < used, 1.0, 0.0)
            row, base, shift = spot(slot)
            rows = pl.ds(member * win, win)
            columns = slice(member * win, (member + 1) * win)
            re = (returned[:win, columns] - waves_buf[rows, :win].astype(jnp.float32)) * weight
            im = (returned[win:, columns] - waves_buf[rows, win:].astype(jnp.float32)) * weight
            add_at(0, row, base, shift, pr * re + pi * im)
            add_at(1, row, base, shift, pr * im - pi * re)
            if with_light:
                add_at(2, row, base, shift, (pr * pr + pi * pi) * weight)
            else:
                ore, oim = patch_buf[member, 0], patch_buf[member, 1]
                gradient[0] += ore * re + oim * im
                gradient[1] += ore * im - oim * re


def sweep(with_light, corners, live, ext, probe, amp, ahead, back):
    slots, win = amp.shape[0], amp.shape[1]
    strips, side = ext.shape[1:3]
    vmem = pl.BlockSpec(memory_space=pltpu.VMEM)
    smem = pl.BlockSpec(memory_space=pltpu.SMEM)
    planes = 3 if with_light else 2
    out_shape = [jax.ShapeDtypeStruct((planes, strips, side, win), jnp.float32)]
    scratch = [pltpu.VMEM((GROUP * win, 2 * win), jnp.bfloat16)]
    if not with_light:
        out_shape.append(jax.ShapeDtypeStruct((2, win, win), jnp.float32))
        scratch.append(pltpu.VMEM((GROUP, 2, win, win), jnp.float32))
    return pl.pallas_call(
        functools.partial(sweep_kernel, with_light),
        out_shape=out_shape,
        in_specs=[smem, smem] + [vmem] * 5,
        out_specs=[vmem] * len(out_shape),
        scratch_shapes=scratch,
        name="first_sweep" if with_light else "second_sweep",
    )(corners, live, ext, probe, amp, ahead, back)


def strips_of(value, window):
    planes, rows, columns = value.shape
    return jnp.transpose(value.reshape(planes, rows, columns // window, window), (0, 2, 1, 3))


def extend(current, window):
    right_rim = from_behind(current[:, :, :window], "col", -1)
    lower_rim = from_behind(current[:, :window, :], "row", -1)
    corner_rim = from_behind(
        current[:, :window, :window], ("row", "col"), -(lax.axis_size("col") + 1)
    )
    widened = jnp.concatenate([current, right_rim], 2)
    lower_wide = jnp.concatenate([lower_rim, corner_rim], 2)
    return strips_of(jnp.concatenate([widened, lower_wide], 1), window)


def fold(deposit, window):
    deposit = jnp.transpose(deposit, (0, 2, 1, 3)).reshape(deposit.shape[0], deposit.shape[2], -1)
    tile_size = deposit.shape[1] - window
    spilled = from_behind(deposit[:, tile_size:, :tile_size], "row", 1)
    right_part = from_behind(deposit[:, :tile_size, tile_size:], "col", 1)
    corner_part = from_behind(
        deposit[:, tile_size:, tile_size:], ("row", "col"), lax.axis_size("col") + 1
    )
    result = deposit[:, :tile_size, :tile_size]
    result = result.at[:, :window, :].add(spilled)
    result = result.at[:, :, :window].add(right_part)
    return result.at[:, :window, :window].add(corner_part)


def on_device(object_field, probe, amplitude, corners, live_count):
    slots = amplitude.shape[2]
    window = probe.shape[1]
    amp = amplitude.reshape(slots, window, window)
    corners = corners.reshape(2, slots)
    live = live_count.reshape(1)
    ahead, back = dft_tables(window)
    (deposit,) = sweep(True, corners, live, extend(object_field, window), probe, amp, ahead, back)
    first_pass = fold(deposit, window)
    denominator = first_pass[2] + 4.0
    updated = object_field + first_pass[:2] / denominator
    deposit, gradient = sweep(
        False, corners, live, extend(updated, window), probe, amp, ahead, back
    )
    refined_object = updated + fold(deposit, window) / denominator
    summed = lax.psum(gradient, ("row", "col"))
    spread = jnp.sqrt(jnp.mean(summed[0] * summed[0] + summed[1] * summed[1]) + 1e-06)
    new_probe = probe + summed / spread
    return (refined_object, new_probe)


def solution(mesh):
    in_specs = (
        P(None, "row", "col"),
        P(),
        P("row", "col", None, None, None),
        P(None, "row", "col", None),
        P("row", "col"),
    )
    out_specs = (P(None, "row", "col"), P())
    return jax.shard_map(
        on_device, mesh=mesh, in_specs=in_specs, out_specs=out_specs, check_vma=False
    )
```

```python
import functools
import math

import jax
import jax.numpy as jnp
import numpy as np
from jax import lax
from jax.experimental import pallas as pl
from jax.experimental.pallas import tpu as pltpu
from jax.sharding import PartitionSpec as P

GROUP = 4


def dft_tables(window):
    indices = np.arange(window, dtype=np.int32)
    phase_index = indices[:, None] * indices[None, :] % window
    angles = phase_index.astype(np.float32) * np.float32(2.0 * math.pi / window)
    norming = np.float32(1.0 / math.sqrt(window))
    cosines = np.cos(angles) * norming
    sines = np.sin(angles) * norming
    forward = np.block([[cosines, -sines], [sines, cosines]]).astype(np.float32)
    return (jnp.asarray(forward, jnp.bfloat16), jnp.asarray(forward.T.copy(), jnp.bfloat16))


def dot(left, right):
    return jnp.dot(left, right, preferred_element_type=jnp.float32)


def sweep_kernel(with_light, corners, live, ext, probe, amp, ahead, back, deposit, *rest):
    if with_light:
        waves_buf = rest[0]
    else:
        gradient, waves_buf, patch_buf = rest
        gradient[...] = jnp.zeros_like(gradient)
    slots, win = amp.shape[0], amp.shape[1]
    deposit[...] = jnp.zeros_like(deposit)
    lane = lax.broadcasted_iota(jnp.int32, (win, win), 1)
    used = live[0]

    def spot(slot):
        row, col = corners[0, slot], corners[1, slot]
        base = col // win
        return row, base, col - base * win

    def add_at(plane, row, base, shift, value):
        turned = pltpu.roll(value, shift, 1)
        left = jnp.where(lane >= shift, turned, 0.0)
        right = jnp.where(lane >= shift, 0.0, turned)
        for offset, part in ((0, left), (1, right)):
            at = (plane, base + offset, pl.ds(row, win))
            deposit[at] = deposit[at] + part

    @pl.loop(0, (used + GROUP - 1) // GROUP)
    def _(turn):
        first = turn * GROUP
        pr, pi = probe[0], probe[1]
        for member in range(GROUP):
            row, base, shift = spot(first + member)
            parts = []
            for plane in range(2):
                left = ext[plane, base, pl.ds(row, win)]
                right = ext[plane, base + 1, pl.ds(row, win)]
                mixed = jnp.where(lane >= shift, left, right)
                parts.append(pltpu.roll(mixed, lax.rem(win - shift, win), 1))
            re, im = parts
            if not with_light:
                patch_buf[member, 0] = re
                patch_buf[member, 1] = im
            rows = pl.ds(member * win, win)
            waves_buf[rows, :win] = (pr * re - pi * im).astype(jnp.bfloat16)
            waves_buf[rows, win:] = (pr * im + pi * re).astype(jnp.bfloat16)
        half = dot(waves_buf[...], ahead[...]).astype(jnp.bfloat16)

        def upright(value):
            columns = []
            for member in range(GROUP):
                block = value[member * win : (member + 1) * win]
                columns.append(jnp.concatenate([block[:, :win], block[:, win:]], 0))
            return jnp.concatenate(columns, 1)

        spectrum = dot(back[...], upright(half))
        projected = []
        for member in range(GROUP):
            re = spectrum[:win, member * win : (member + 1) * win]
            im = spectrum[win:, member * win : (member + 1) * win]
            scale = amp[first + member].astype(jnp.float32) * lax.rsqrt(
                jnp.maximum(re * re + im * im, 0.25)
            )
            projected.append(
                jnp.concatenate(
                    [(re * scale).astype(jnp.bfloat16), (im * scale).astype(jnp.bfloat16)], 1
                )
            )
        half_back = dot(jnp.concatenate(projected, 0), back[...]).astype(jnp.bfloat16)
        returned = dot(ahead[...], upright(half_back))
        for member in range(GROUP):
            slot = first + member
            weight = jnp.where(slot < used, 1.0, 0.0)
            row, base, shift = spot(slot)
            rows = pl.ds(member * win, win)
            columns = slice(member * win, (member + 1) * win)
            re = (returned[:win, columns] - waves_buf[rows, :win].astype(jnp.float32)) * weight
            im = (returned[win:, columns] - waves_buf[rows, win:].astype(jnp.float32)) * weight
            add_at(0, row, base, shift, pr * re + pi * im)
            add_at(1, row, base, shift, pr * im - pi * re)
            if with_light:
                add_at(2, row, base, shift, (pr * pr + pi * pi) * weight)
            else:
                ore, oim = patch_buf[member, 0], patch_buf[member, 1]
                gradient[0] += ore * re + oim * im
                gradient[1] += ore * im - oim * re


def sweep(with_light, corners, live, ext, probe, amp, ahead, back):
    slots, win = amp.shape[0], amp.shape[1]
    strips, side = ext.shape[1:3]
    vmem = pl.BlockSpec(memory_space=pltpu.VMEM)
    smem = pl.BlockSpec(memory_space=pltpu.SMEM)
    planes = 3 if with_light else 2
    out_shape = [jax.ShapeDtypeStruct((planes, strips, side, win), jnp.float32)]
    scratch = [pltpu.VMEM((GROUP * win, 2 * win), jnp.bfloat16)]
    if not with_light:
        out_shape.append(jax.ShapeDtypeStruct((2, win, win), jnp.float32))
        scratch.append(pltpu.VMEM((GROUP, 2, win, win), jnp.float32))
    return pl.pallas_call(
        functools.partial(sweep_kernel, with_light),
        out_shape=out_shape,
        in_specs=[smem, smem] + [vmem] * 5,
        out_specs=[vmem] * len(out_shape),
        scratch_shapes=scratch,
        name="first_sweep" if with_light else "second_sweep",
    )(corners, live, ext, probe, amp, ahead, back)


MESH = pl.DeviceIdType.MESH


class Place:
    def __init__(self, rows, cols):
        self.row, self.col = lax.axis_index("row"), lax.axis_index("col")
        self.rows, self.cols = rows, cols

    def at(self, down, right):
        return (
            lax.rem(self.row + down + self.rows, self.rows),
            lax.rem(self.col + right + self.cols, self.cols),
        )

    def inside(self, down, right):
        checks = []
        if down:
            checks.append(self.row < self.rows - 1 if down > 0 else self.row > 0)
        if right:
            checks.append(self.col < self.cols - 1 if right > 0 else self.col > 0)
        return checks[0] if len(checks) == 1 else jnp.logical_and(*checks)


def greet(place, steps):
    barrier = pltpu.get_barrier_semaphore()
    for step in steps:

        @pl.when(place.inside(*step))
        def _():
            pl.semaphore_signal(barrier, inc=1, device_id=place.at(*step), device_id_type=MESH)

    return barrier


def meet(place, barrier, steps, others=0):
    for step in steps:
        others = others + jnp.where(place.inside(*step), 1, 0)
    pl.semaphore_wait(barrier, others)


NEAR = ((0, -1), (-1, 0), (-1, -1), (0, 1), (1, 0), (1, 1))


class Shift:
    def __init__(self, place, step, source, target, sems, index):
        self.copy = pltpu.make_async_remote_copy(
            src_ref=source,
            dst_ref=target,
            send_sem=sems.at[0, index],
            recv_sem=sems.at[1, index],
            device_id=place.at(*step),
            device_id_type=MESH,
        )
        self.sends = place.inside(*step)
        self.receives = place.inside(-step[0], -step[1])

    def start(self):
        pl.when(self.sends)(self.copy.start)

    def wait_send(self):
        pl.when(self.sends)(self.copy.wait_send)


def rim_shifts(place, field, ext, sems, win):
    tile = ext.shape[2] - win
    return [
        Shift(place, (0, -1), field(0, tile), ext.at[:, 2, pl.ds(0, tile)], sems, 0),
        Shift(place, (-1, -1), field(0, win), ext.at[:, 2, pl.ds(tile, win)], sems, 1),
        Shift(place, (-1, 0), field(0, win), ext.at[:, 0, pl.ds(tile, win)], sems, 2),
        Shift(place, (-1, 0), field(1, win), ext.at[:, 1, pl.ds(tile, win)], sems, 3),
    ]


def spill_shifts(place, deposit, right_in, low_in, corner_in, sems, win):
    tile = deposit.shape[2] - win
    return [
        Shift(place, (0, 1), deposit.at[:, 2, pl.ds(0, tile)], right_in, sems, 0),
        Shift(place, (1, 1), deposit.at[:, 2, pl.ds(tile, win)], corner_in, sems, 1),
        Shift(place, (1, 0), deposit.at[:, pl.ds(0, 2), pl.ds(tile, win)], low_in, sems, 2),
    ]


def finish(shifts):
    for shift in shifts:
        pl.when(shift.receives)(shift.copy.wait_recv)
    for shift in shifts:
        shift.wait_send()


def extend_kernel(rows, cols, obj, ext, sems):
    win = ext.shape[3]
    tile = ext.shape[2] - win
    place = Place(rows, cols)
    barrier = greet(place, NEAR)
    for strip in range(2):
        ext[:, strip, :tile] = obj[:, :, strip * win : (strip + 1) * win]
    meet(place, barrier, NEAR)

    def field(strip, height):
        return obj.at[:, pl.ds(0, height), pl.ds(strip * win, win)]

    shifts = rim_shifts(place, field, ext, sems, win)
    for shift in shifts:
        shift.start()
    finish(shifts)


def update_kernel(
    rows, cols, spread, obj, ext, inverse, right_in, low_in, corner_in, total, sems, rim_sems
):
    win = ext.shape[3]
    tile = ext.shape[2] - win
    place = Place(rows, cols)
    barrier = greet(place, NEAR)
    meet(place, barrier, NEAR)
    shifts = spill_shifts(place, spread, right_in, low_in, corner_in, sems, win)
    for shift in shifts:
        shift.start()
    for strip in range(2):
        total[:, strip] = spread[:, strip, :tile]
    side, corner, low = shifts

    @pl.when(low.receives)
    def _():
        low.copy.wait_recv()
        for strip in range(2):
            total[:, strip, :win] += low_in[:, strip]

    @pl.when(side.receives)
    def _():
        side.copy.wait_recv()
        total[:, 0] += right_in[...]

    @pl.when(corner.receives)
    def _():
        corner.copy.wait_recv()
        total[:, 0, :win] += corner_in[...]

    rims = rim_shifts(
        place, lambda strip, height: ext.at[:, strip, pl.ds(0, height)], ext, rim_sems, win
    )
    for strip in range(2):
        share = 1.0 / (total[2, strip] + 4.0)
        inverse[strip] = share
        for plane in range(2):
            ext[plane, strip, :tile] = (
                obj[plane, :, strip * win : (strip + 1) * win] + total[plane, strip] * share
            )
        for rim in rims[:3] if strip == 0 else rims[3:]:
            rim.start()
    for shift in shifts:
        shift.wait_send()
    finish(rims)


def last_kernel(
    rows,
    cols,
    spread,
    ext,
    inverse,
    gradient,
    probe,
    refined,
    new_probe,
    right_in,
    low_in,
    corner_in,
    part_in,
    peer_in,
    whole,
    own,
    sems,
    part_sems,
    peer_sems,
    whole_sems,
):
    win = ext.shape[3]
    tile = ext.shape[2] - win
    place = Place(rows, cols)
    diagonal = ((-1, -1), (1, 1))
    barrier = greet(place, diagonal)
    col_peers = [place.at(0, step) for step in range(1, cols)]
    row_peers = [place.at(step, 0) for step in range(1, rows)]
    for peer in col_peers + row_peers:
        pl.semaphore_signal(barrier, inc=1, device_id=peer, device_id_type=MESH)
    meet(place, barrier, diagonal, cols + rows - 2)
    height = whole.shape[0] // cols

    def piece(index):
        return pl.ds(pl.multiple_of(index * height, height), height)

    def send(source, target, pair, index, peer):
        copy = pltpu.make_async_remote_copy(
            src_ref=source,
            dst_ref=target,
            send_sem=pair.at[0, index],
            recv_sem=pair.at[1, index],
            device_id=peer,
            device_id_type=MESH,
        )
        copy.start()
        return copy

    parts = [
        send(gradient.at[piece(peer[1])], part_in.at[index], part_sems, index, peer)
        for index, peer in enumerate(col_peers)
    ]
    shifts = spill_shifts(place, spread, right_in, low_in, corner_in, sems, win)
    for shift in shifts:
        shift.start()
    summed = gradient[piece(place.col)]
    for index, copy in enumerate(parts):
        copy.wait_recv()
        summed = summed + part_in[index]
    own[...] = summed
    peer_in[place.row] = summed
    peers = [
        send(own, peer_in.at[place.row], peer_sems, index, peer)
        for index, peer in enumerate(row_peers)
    ]
    for copy in peers:
        copy.wait_recv()
    summed = peer_in[0]
    for index in range(1, rows):
        summed = summed + peer_in[index]
    whole[piece(place.col)] = summed
    gathers = [
        send(whole.at[piece(place.col)], whole.at[piece(place.col)], whole_sems, index, peer)
        for index, peer in enumerate(col_peers)
    ]
    for strip in range(2):
        for plane in range(2):
            refined[plane, :, strip * win : (strip + 1) * win] = spread[plane, strip, :tile]
    side, corner, low = shifts

    @pl.when(low.receives)
    def _():
        low.copy.wait_recv()
        for strip in range(2):
            refined[:, :win, strip * win : (strip + 1) * win] += low_in[:, strip]

    @pl.when(side.receives)
    def _():
        side.copy.wait_recv()
        refined[:, :, :win] += right_in[...]

    @pl.when(corner.receives)
    def _():
        corner.copy.wait_recv()
        refined[:, :win, :win] += corner_in[...]

    for strip in range(2):
        columns = slice(strip * win, (strip + 1) * win)
        for plane in range(2):
            refined[plane, :, columns] = (
                ext[plane, strip, :tile] + refined[plane, :, columns] * inverse[strip]
            )
    for copy in gathers:
        copy.wait_recv()
    total = whole[...]
    power = jnp.sum(total * total, axis=(0, 1), keepdims=True) / (total.shape[0] // 2 * win)
    new_probe[...] = probe[...] + total * lax.rsqrt(power + 1e-06)
    for copy in parts + peers + gathers:
        copy.wait_send()
    for shift in shifts:
        shift.wait_send()


def remote_call(kernel, ident, out_shape, scratch, operands):
    vmem = pl.BlockSpec(memory_space=pltpu.VMEM)
    return pl.pallas_call(
        kernel,
        out_shape=out_shape,
        in_specs=[vmem] * len(operands),
        out_specs=[vmem] * len(out_shape),
        scratch_shapes=scratch,
        compiler_params=pltpu.CompilerParams(collective_id=ident, has_side_effects=True),
    )(*operands)


def on_device(rows, cols, object_field, probe, amplitude, corners, live_count):
    slots = amplitude.shape[2]
    win = probe.shape[1]
    tile = object_field.shape[1]
    amp = amplitude.reshape(slots, win, win)
    corners = corners.reshape(2, slots)
    live = live_count.reshape(1)
    ahead, back = dft_tables(win)
    f32 = jnp.float32
    sem = pltpu.SemaphoreType.DMA
    ext_shape = jax.ShapeDtypeStruct((2, tile // win + 1, tile + win, win), f32)

    def inboxes(planes):
        return [
            pltpu.VMEM((planes, tile, win), f32),
            pltpu.VMEM((planes, 2, win, win), f32),
            pltpu.VMEM((planes, win, win), f32),
        ]

    (ext,) = remote_call(
        functools.partial(extend_kernel, rows, cols), 0, [ext_shape], [sem((2, 4))], [object_field]
    )
    (spread,) = sweep(True, corners, live, ext, probe, amp, ahead, back)
    ext, inverse = remote_call(
        functools.partial(update_kernel, rows, cols),
        1,
        [ext_shape, jax.ShapeDtypeStruct((2, tile, win), f32)],
        inboxes(3) + [pltpu.VMEM((3, 2, tile, win), f32), sem((2, 3)), sem((2, 4))],
        [spread, object_field],
    )
    spread, gradient = sweep(False, corners, live, ext, probe, amp, ahead, back)
    flat = (2 * win, win)
    height = 2 * win // cols
    refined, new_probe = remote_call(
        functools.partial(last_kernel, rows, cols),
        2,
        [jax.ShapeDtypeStruct(object_field.shape, f32), jax.ShapeDtypeStruct(flat, f32)],
        inboxes(2)
        + [
            pltpu.VMEM((cols - 1, height, win), f32),
            pltpu.VMEM((rows, height, win), f32),
            pltpu.VMEM(flat, f32),
            pltpu.VMEM((height, win), f32),
            sem((2, 3)),
            sem((2, cols - 1)),
            sem((2, rows - 1)),
            sem((2, cols - 1)),
        ],
        [spread, ext, inverse, gradient.reshape(flat), probe.reshape(flat)],
    )
    return (refined, new_probe.reshape(probe.shape))


def solution(mesh):
    in_specs = (
        P(None, "row", "col"),
        P(),
        P("row", "col", None, None, None),
        P(None, "row", "col", None),
        P("row", "col"),
    )
    out_specs = (P(None, "row", "col"), P())
    return jax.shard_map(
        functools.partial(on_device, mesh.shape["row"], mesh.shape["col"]), mesh=mesh, in_specs=in_specs, out_specs=out_specs, check_vma=False
    )
```

```python
import functools
import math

import jax
import jax.numpy as jnp
import numpy as np
from jax import lax
from jax.experimental import pallas as pl
from jax.experimental.pallas import tpu as pltpu
from jax.sharding import PartitionSpec as P

GROUP = 4


def dft_tables(window):
    indices = np.arange(window, dtype=np.int32)
    phase_index = indices[:, None] * indices[None, :] % window
    angles = phase_index.astype(np.float32) * np.float32(2.0 * math.pi / window)
    norming = np.float32(1.0 / math.sqrt(window))
    cosines = np.cos(angles) * norming
    sines = np.sin(angles) * norming
    forward = np.block([[cosines, -sines], [sines, cosines]]).astype(np.float32)
    return (jnp.asarray(forward, jnp.bfloat16), jnp.asarray(forward.T.copy(), jnp.bfloat16))


def dot(left, right):
    return jnp.dot(left, right, preferred_element_type=jnp.float32)


def sweep_kernel(with_light, corners, live, ext, probe, amp, ahead, back, deposit, *rest):
    side_out, low_out, corner_out = rest[:3]
    if with_light:
        waves_buf = rest[3]
    else:
        gradient, narrow, waves_buf, patch_buf = rest[3:]
        gradient[...] = jnp.zeros_like(gradient)
    slots, win = amp.shape[0], amp.shape[1]
    deposit[...] = jnp.zeros_like(deposit)
    lane = lax.broadcasted_iota(jnp.int32, (win, win), 1)
    used = live[0]

    def spot(slot):
        row, col = corners[0, slot], corners[1, slot]
        base = col // win
        return row, base, col - base * win

    def add_at(plane, row, base, shift, value):
        turned = pltpu.roll(value, shift, 1)
        left = jnp.where(lane >= shift, turned, 0.0)
        right = jnp.where(lane >= shift, 0.0, turned)
        for offset, part in ((0, left), (1, right)):
            at = (plane, base + offset, pl.ds(row, win))
            deposit[at] = deposit[at] + part

    @pl.loop(0, (used + GROUP - 1) // GROUP)
    def _(turn):
        first = turn * GROUP
        pr, pi = probe[0], probe[1]
        for member in range(GROUP):
            row, base, shift = spot(first + member)
            parts = []
            for plane in range(2):
                left = ext[plane, base, pl.ds(row, win)]
                right = ext[plane, base + 1, pl.ds(row, win)]
                mixed = jnp.where(lane >= shift, left, right)
                parts.append(pltpu.roll(mixed, lax.rem(win - shift, win), 1))
            re, im = parts
            if not with_light:
                patch_buf[member, 0] = re
                patch_buf[member, 1] = im
            rows = pl.ds(member * win, win)
            waves_buf[rows, :win] = (pr * re - pi * im).astype(jnp.bfloat16)
            waves_buf[rows, win:] = (pr * im + pi * re).astype(jnp.bfloat16)
        half = dot(waves_buf[...], ahead[...]).astype(jnp.bfloat16)

        def upright(value):
            columns = []
            for member in range(GROUP):
                block = value[member * win : (member + 1) * win]
                columns.append(jnp.concatenate([block[:, :win], block[:, win:]], 0))
            return jnp.concatenate(columns, 1)

        spectrum = dot(back[...], upright(half))
        projected = []
        for member in range(GROUP):
            re = spectrum[:win, member * win : (member + 1) * win]
            im = spectrum[win:, member * win : (member + 1) * win]
            scale = amp[first + member].astype(jnp.float32) * lax.rsqrt(
                jnp.maximum(re * re + im * im, 0.25)
            )
            projected.append(
                jnp.concatenate(
                    [(re * scale).astype(jnp.bfloat16), (im * scale).astype(jnp.bfloat16)], 1
                )
            )
        half_back = dot(jnp.concatenate(projected, 0), back[...]).astype(jnp.bfloat16)
        returned = dot(ahead[...], upright(half_back))
        for member in range(GROUP):
            slot = first + member
            weight = jnp.where(slot < used, 1.0, 0.0)
            row, base, shift = spot(slot)
            rows = pl.ds(member * win, win)
            columns = slice(member * win, (member + 1) * win)
            re = (returned[:win, columns] - waves_buf[rows, :win].astype(jnp.float32)) * weight
            im = (returned[win:, columns] - waves_buf[rows, win:].astype(jnp.float32)) * weight
            add_at(0, row, base, shift, pr * re + pi * im)
            add_at(1, row, base, shift, pr * im - pi * re)
            if with_light:
                add_at(2, row, base, shift, (pr * pr + pi * pi) * weight)
            else:
                ore, oim = patch_buf[member, 0], patch_buf[member, 1]
                gradient[0] += ore * re + oim * im
                gradient[1] += ore * im - oim * re

    tile = deposit.shape[2] - win
    side_out[...] = deposit[:, 2, :tile].astype(jnp.bfloat16)
    low_out[...] = deposit[:, :2, tile:].astype(jnp.bfloat16)
    corner_out[...] = deposit[:, 2, tile:].astype(jnp.bfloat16)
    if not with_light:
        narrow[...] = gradient[...].astype(jnp.bfloat16)


def spill_shapes(planes, tile, win):
    return [(planes, tile, win), (planes, 2, win, win), (planes, win, win)]


def sweep(with_light, corners, live, ext, probe, amp, ahead, back):
    slots, win = amp.shape[0], amp.shape[1]
    strips, side = ext.shape[1:3]
    vmem = pl.BlockSpec(memory_space=pltpu.VMEM)
    smem = pl.BlockSpec(memory_space=pltpu.SMEM)
    planes = 3 if with_light else 2
    out_shape = [jax.ShapeDtypeStruct((planes, strips, side, win), jnp.float32)]
    for shape in spill_shapes(planes, side - win, win):
        out_shape.append(jax.ShapeDtypeStruct(shape, jnp.bfloat16))
    scratch = [pltpu.VMEM((GROUP * win, 2 * win), jnp.bfloat16)]
    if not with_light:
        out_shape.append(jax.ShapeDtypeStruct((2, win, win), jnp.float32))
        out_shape.append(jax.ShapeDtypeStruct((2, win, win), jnp.bfloat16))
        scratch.append(pltpu.VMEM((GROUP, 2, win, win), jnp.float32))
    return pl.pallas_call(
        functools.partial(sweep_kernel, with_light),
        out_shape=out_shape,
        in_specs=[smem, smem] + [vmem] * 5,
        out_specs=[vmem] * len(out_shape),
        scratch_shapes=scratch,
        name="first_sweep" if with_light else "second_sweep",
    )(corners, live, ext, probe, amp, ahead, back)


MESH = pl.DeviceIdType.MESH


class Place:
    def __init__(self, rows, cols):
        self.row, self.col = lax.axis_index("row"), lax.axis_index("col")
        self.rows, self.cols = rows, cols

    def at(self, down, right):
        return (
            lax.rem(self.row + down + self.rows, self.rows),
            lax.rem(self.col + right + self.cols, self.cols),
        )

    def inside(self, down, right):
        checks = []
        if down:
            checks.append(self.row < self.rows - 1 if down > 0 else self.row > 0)
        if right:
            checks.append(self.col < self.cols - 1 if right > 0 else self.col > 0)
        return checks[0] if len(checks) == 1 else jnp.logical_and(*checks)


def greet(place, steps):
    barrier = pltpu.get_barrier_semaphore()
    for step in steps:

        @pl.when(place.inside(*step))
        def _():
            pl.semaphore_signal(barrier, inc=1, device_id=place.at(*step), device_id_type=MESH)

    return barrier


def meet(place, barrier, steps, others=0):
    for step in steps:
        others = others + jnp.where(place.inside(*step), 1, 0)
    pl.semaphore_wait(barrier, others)


NEAR = ((0, -1), (-1, 0), (-1, -1), (0, 1), (1, 0), (1, 1))


class Shift:
    def __init__(self, place, step, source, target, sems, index):
        self.copy = pltpu.make_async_remote_copy(
            src_ref=source,
            dst_ref=target,
            send_sem=sems.at[0, index],
            recv_sem=sems.at[1, index],
            device_id=place.at(*step),
            device_id_type=MESH,
        )
        self.sends = place.inside(*step)
        self.receives = place.inside(-step[0], -step[1])

    def start(self):
        pl.when(self.sends)(self.copy.start)

    def wait_send(self):
        pl.when(self.sends)(self.copy.wait_send)


def box_shifts(place, down, side, low, corner, sems):
    return [
        Shift(place, (0, down), *side, sems, 0),
        Shift(place, (down, down), *corner, sems, 1),
        Shift(place, (down, 0), *low, sems, 2),
    ]


def finish_sends(shifts):
    for shift in shifts:
        shift.wait_send()


def arrive(shifts, side, low, corner):
    for shift, action in zip((shifts[2], shifts[0], shifts[1]), (low, side, corner)):

        @pl.when(shift.receives)
        def _():
            shift.copy.wait_recv()
            action()


def fill_rims(shifts, ext, side_in, low_in, corner_in):
    win = ext.shape[3]
    tile = ext.shape[2] - win

    def low():
        ext[:, :2, tile:] = low_in[...].astype(jnp.float32)

    def side():
        ext[:, 2, :tile] = side_in[...].astype(jnp.float32)

    def corner():
        ext[:, 2, tile:] = corner_in[...].astype(jnp.float32)

    arrive(shifts, side, low, corner)


def add_spills(shifts, total, side_in, low_in, corner_in):
    win = total.shape[3]

    def low():
        total[:, :, :win] += low_in[...].astype(jnp.float32)

    def side():
        total[:, 0] += side_in[...].astype(jnp.float32)

    def corner():
        total[:, 0, :win] += corner_in[...].astype(jnp.float32)

    arrive(shifts, side, low, corner)


def rim_boxes(place, outs, ins, win, sems):
    side_out, low_out = outs
    side_in, low_in, corner_in = ins
    return box_shifts(
        place,
        -1,
        (side_out, side_in),
        (low_out, low_in),
        (side_out.at[:, pl.ds(0, win)], corner_in),
        sems,
    )


def extend_kernel(rows, cols, obj, ext, side_out, low_out, side_in, low_in, corner_in, sems):
    win = ext.shape[3]
    tile = ext.shape[2] - win
    place = Place(rows, cols)
    barrier = greet(place, NEAR)
    side_out[...] = obj[:, :, :win].astype(jnp.bfloat16)
    for strip in range(2):
        low_out[:, strip] = obj[:, :win, strip * win : (strip + 1) * win].astype(jnp.bfloat16)
    meet(place, barrier, NEAR)
    shifts = rim_boxes(place, (side_out, low_out), (side_in, low_in, corner_in), win, sems)
    for shift in shifts:
        shift.start()
    for strip in range(2):
        ext[:, strip, :tile] = obj[:, :, strip * win : (strip + 1) * win]
    fill_rims(shifts, ext, side_in, low_in, corner_in)
    finish_sends(shifts)


def update_kernel(rows, cols, *refs):
    spread, side_spill, low_spill, corner_spill, obj, ext, inverse = refs[:7]
    side_got, low_got, corner_got, side_out, low_out, side_in, low_in, corner_in = refs[7:15]
    total, sems, rim_sems = refs[15:]
    win = ext.shape[3]
    tile = ext.shape[2] - win
    place = Place(rows, cols)
    barrier = greet(place, NEAR)
    meet(place, barrier, NEAR)
    spills = box_shifts(
        place,
        1,
        (side_spill, side_got),
        (low_spill, low_got),
        (corner_spill, corner_got),
        sems,
    )
    for shift in spills:
        shift.start()
    total[...] = spread[:, :2, :tile]
    add_spills(spills, total, side_got, low_got, corner_got)
    rims = rim_boxes(place, (side_out, low_out), (side_in, low_in, corner_in), win, rim_sems)
    for strip in range(2):
        share = 1.0 / (total[2, strip] + 4.0)
        for plane in range(2):
            fresh = obj[plane, :, strip * win : (strip + 1) * win] + total[plane, strip] * share
            if strip == 0:
                side_out[plane] = fresh.astype(jnp.bfloat16)
            low_out[plane, strip] = fresh[:win].astype(jnp.bfloat16)
            ext[plane, strip, :tile] = fresh
        inverse[strip] = share
        for rim in rims[:2] if strip == 0 else rims[2:]:
            rim.start()
    finish_sends(spills)
    fill_rims(rims, ext, side_in, low_in, corner_in)
    finish_sends(rims)


def last_kernel(rows, cols, *refs):
    spread, side_spill, low_spill, corner_spill, ext, inverse, gradient, narrow, probe = refs[:9]
    refined, new_probe, side_got, low_got, corner_got, total = refs[9:15]
    part_in, peer_in, whole, own, sems, part_sems, peer_sems, whole_sems = refs[15:]
    win = ext.shape[3]
    tile = ext.shape[2] - win
    place = Place(rows, cols)
    diagonal = ((-1, -1), (1, 1))
    barrier = greet(place, diagonal)
    col_peers = [place.at(0, step) for step in range(1, cols)]
    row_peers = [place.at(step, 0) for step in range(1, rows)]
    for peer in col_peers + row_peers:
        pl.semaphore_signal(barrier, inc=1, device_id=peer, device_id_type=MESH)
    meet(place, barrier, diagonal, cols + rows - 2)
    height = whole.shape[0] // rows

    def piece(index):
        return pl.ds(pl.multiple_of(index * height, height), height)

    def send(source, target, pair, index, peer):
        copy = pltpu.make_async_remote_copy(
            src_ref=source,
            dst_ref=target,
            send_sem=pair.at[0, index],
            recv_sem=pair.at[1, index],
            device_id=peer,
            device_id_type=MESH,
        )
        copy.start()
        return copy

    parts = [
        send(narrow.at[piece(peer[0])], part_in.at[index], part_sems, index, peer)
        for index, peer in enumerate(row_peers)
    ]
    spills = box_shifts(
        place,
        1,
        (side_spill, side_got),
        (low_spill, low_got),
        (corner_spill, corner_got),
        sems,
    )
    for shift in spills:
        shift.start()
    summed = gradient[piece(place.row)]
    for index, copy in enumerate(parts):
        copy.wait_recv()
        summed = summed + part_in[index].astype(jnp.float32)
    own[...] = summed.astype(jnp.bfloat16)
    peer_in[place.col] = summed.astype(jnp.bfloat16)
    peers = [
        send(own, peer_in.at[place.col], peer_sems, index, peer)
        for index, peer in enumerate(col_peers)
    ]
    total[...] = spread[:, :2, :tile]
    for copy in peers:
        copy.wait_recv()
    summed = peer_in[0].astype(jnp.float32)
    for index in range(1, cols):
        summed = summed + peer_in[index].astype(jnp.float32)
    whole[piece(place.row)] = summed
    gathers = [
        send(whole.at[piece(place.row)], whole.at[piece(place.row)], whole_sems, index, peer)
        for index, peer in enumerate(row_peers)
    ]
    add_spills(spills, total, side_got, low_got, corner_got)
    for strip in range(2):
        for plane in range(2):
            refined[plane, :, strip * win : (strip + 1) * win] = (
                ext[plane, strip, :tile] + total[plane, strip] * inverse[strip]
            )
    for copy in gathers:
        copy.wait_recv()
    value = whole[...]
    power = jnp.sum(value * value, axis=(0, 1), keepdims=True) / (value.shape[0] // 2 * win)
    new_probe[...] = probe[...] + value * lax.rsqrt(power + 1e-06)
    for copy in parts + peers + gathers:
        copy.wait_send()
    finish_sends(spills)


def remote_call(kernel, ident, out_shape, scratch, operands):
    vmem = pl.BlockSpec(memory_space=pltpu.VMEM)
    return pl.pallas_call(
        kernel,
        out_shape=out_shape,
        in_specs=[vmem] * len(operands),
        out_specs=[vmem] * len(out_shape),
        scratch_shapes=scratch,
        compiler_params=pltpu.CompilerParams(collective_id=ident, has_side_effects=True),
    )(*operands)


def on_device(rows, cols, object_field, probe, amplitude, corners, live_count):
    slots = amplitude.shape[2]
    win = probe.shape[1]
    tile = object_field.shape[1]
    amp = amplitude.reshape(slots, win, win)
    corners = corners.reshape(2, slots)
    live = live_count.reshape(1)
    ahead, back = dft_tables(win)
    f32, b16 = jnp.float32, jnp.bfloat16
    sem = pltpu.SemaphoreType.DMA
    ext_shape = jax.ShapeDtypeStruct((2, tile // win + 1, tile + win, win), f32)

    def boxes(planes, count=3):
        return [pltpu.VMEM(shape, b16) for shape in spill_shapes(planes, tile, win)[:count]]

    (ext,) = remote_call(
        functools.partial(extend_kernel, rows, cols),
        0,
        [ext_shape],
        boxes(2, 2) + boxes(2) + [sem((2, 3))],
        [object_field],
    )
    spread, *spills = sweep(True, corners, live, ext, probe, amp, ahead, back)
    ext, inverse = remote_call(
        functools.partial(update_kernel, rows, cols),
        1,
        [ext_shape, jax.ShapeDtypeStruct((2, tile, win), f32)],
        boxes(3)
        + boxes(2, 2)
        + boxes(2)
        + [pltpu.VMEM((3, 2, tile, win), f32), sem((2, 3)), sem((2, 3))],
        [spread, *spills, object_field],
    )
    spread, *spills, gradient, narrow = sweep(False, corners, live, ext, probe, amp, ahead, back)
    flat = (2 * win, win)
    height = 2 * win // rows
    refined, new_probe = remote_call(
        functools.partial(last_kernel, rows, cols),
        2,
        [jax.ShapeDtypeStruct(object_field.shape, f32), jax.ShapeDtypeStruct(flat, f32)],
        boxes(2)
        + [
            pltpu.VMEM((2, 2, tile, win), f32),
            pltpu.VMEM((rows - 1, height, win), b16),
            pltpu.VMEM((cols, height, win), b16),
            pltpu.VMEM(flat, f32),
            pltpu.VMEM((height, win), b16),
            sem((2, 3)),
            sem((2, rows - 1)),
            sem((2, cols - 1)),
            sem((2, rows - 1)),
        ],
        [
            spread,
            *spills,
            ext,
            inverse,
            gradient.reshape(flat),
            narrow.reshape(flat),
            probe.reshape(flat),
        ],
    )
    return (refined, new_probe.reshape(probe.shape))


def solution(mesh):
    in_specs = (
        P(None, "row", "col"),
        P(),
        P("row", "col", None, None, None),
        P(None, "row", "col", None),
        P("row", "col"),
    )
    out_specs = (P(None, "row", "col"), P())
    return jax.shard_map(
        functools.partial(on_device, mesh.shape["row"], mesh.shape["col"]), mesh=mesh, in_specs=in_specs, out_specs=out_specs, check_vma=False
    )
```

```python
import functools
import math

import jax
import jax.numpy as jnp
import numpy as np
from jax import lax
from jax.experimental import pallas as pl
from jax.experimental.pallas import tpu as pltpu
from jax.sharding import PartitionSpec as P

GROUP = 4
GRANT = 12 << 20


def dft_tables(window):
    indices = np.arange(window, dtype=np.int32)
    phase_index = indices[:, None] * indices[None, :] % window
    angles = phase_index.astype(np.float32) * np.float32(2.0 * math.pi / window)
    norming = np.float32(1.0 / math.sqrt(window))
    cosines = np.cos(angles) * norming
    sines = np.sin(angles) * norming
    forward = np.block([[cosines, -sines], [sines, cosines]]).astype(np.float32)
    return (jnp.asarray(forward, jnp.bfloat16), jnp.asarray(forward.T.copy(), jnp.bfloat16))


def dot(left, right):
    return jnp.dot(left, right, preferred_element_type=jnp.float32)


def sweep_kernel(with_light, corners, live, ext, probe, amp, ahead, back, deposit, *rest):
    side_out, low_out, corner_out = rest[:3]
    if with_light:
        waves_buf = rest[3]
    else:
        gradient, narrow, waves_buf, patch_buf = rest[3:]
        gradient[...] = jnp.zeros_like(gradient)
    slots, win = amp.shape[0], amp.shape[1]
    deposit[...] = jnp.zeros_like(deposit)
    lane = lax.broadcasted_iota(jnp.int32, (win, win), 1)
    used = live[0]

    def spot(slot):
        row, col = corners[0, slot], corners[1, slot]
        base = col // win
        return row, base, col - base * win

    def add_at(plane, row, base, shift, value):
        turned = pltpu.roll(value, shift, 1)
        left = jnp.where(lane >= shift, turned, 0.0)
        right = jnp.where(lane >= shift, 0.0, turned)
        for offset, part in ((0, left), (1, right)):
            at = (plane, base + offset, pl.ds(row, win))
            deposit[at] = deposit[at] + part

    @pl.loop(0, (used + GROUP - 1) // GROUP)
    def _(turn):
        first = turn * GROUP
        pr, pi = probe[0], probe[1]
        for member in range(GROUP):
            row, base, shift = spot(first + member)
            parts = []
            for plane in range(2):
                left = ext[plane, base, pl.ds(row, win)]
                right = ext[plane, base + 1, pl.ds(row, win)]
                mixed = jnp.where(lane >= shift, left, right)
                parts.append(pltpu.roll(mixed, lax.rem(win - shift, win), 1))
            re, im = parts
            if not with_light:
                patch_buf[member, 0] = re
                patch_buf[member, 1] = im
            rows = pl.ds(member * win, win)
            waves_buf[rows, :win] = (pr * re - pi * im).astype(jnp.bfloat16)
            waves_buf[rows, win:] = (pr * im + pi * re).astype(jnp.bfloat16)
        half = dot(waves_buf[...], ahead[...]).astype(jnp.bfloat16)

        def upright(value):
            columns = []
            for member in range(GROUP):
                block = value[member * win : (member + 1) * win]
                columns.append(jnp.concatenate([block[:, :win], block[:, win:]], 0))
            return jnp.concatenate(columns, 1)

        spectrum = dot(back[...], upright(half))
        projected = []
        for member in range(GROUP):
            re = spectrum[:win, member * win : (member + 1) * win]
            im = spectrum[win:, member * win : (member + 1) * win]
            scale = amp[first + member].astype(jnp.float32) * lax.rsqrt(
                jnp.maximum(re * re + im * im, 0.25)
            )
            projected.append(
                jnp.concatenate(
                    [(re * scale).astype(jnp.bfloat16), (im * scale).astype(jnp.bfloat16)], 1
                )
            )
        half_back = dot(jnp.concatenate(projected, 0), back[...]).astype(jnp.bfloat16)
        returned = dot(ahead[...], upright(half_back))
        for member in range(GROUP):
            slot = first + member
            weight = jnp.where(slot < used, 1.0, 0.0)
            row, base, shift = spot(slot)
            rows = pl.ds(member * win, win)
            columns = slice(member * win, (member + 1) * win)
            re = (returned[:win, columns] - waves_buf[rows, :win].astype(jnp.float32)) * weight
            im = (returned[win:, columns] - waves_buf[rows, win:].astype(jnp.float32)) * weight
            add_at(0, row, base, shift, pr * re + pi * im)
            add_at(1, row, base, shift, pr * im - pi * re)
            if with_light:
                add_at(2, row, base, shift, (pr * pr + pi * pi) * weight)
            else:
                ore, oim = patch_buf[member, 0], patch_buf[member, 1]
                gradient[0] += ore * re + oim * im
                gradient[1] += ore * im - oim * re

    tile = deposit.shape[2] - win
    side_out[...] = deposit[:, 2, :tile].astype(jnp.bfloat16)
    low_out[...] = deposit[:, :2, tile:].astype(jnp.bfloat16)
    corner_out[...] = deposit[:, 2, tile:].astype(jnp.bfloat16)
    if not with_light:
        narrow[...] = gradient[...].astype(jnp.bfloat16)


def spill_shapes(planes, tile, win):
    return [(planes, tile, win), (planes, 2, win, win), (planes, win, win)]


def sweep(with_light, corners, live, ext, probe, amp, ahead, back):
    slots, win = amp.shape[0], amp.shape[1]
    strips, side = ext.shape[1:3]
    vmem = pl.BlockSpec(memory_space=pltpu.VMEM)
    smem = pl.BlockSpec(memory_space=pltpu.SMEM)
    planes = 3 if with_light else 2
    out_shape = [jax.ShapeDtypeStruct((planes, strips, side, win), jnp.float32)]
    for shape in spill_shapes(planes, side - win, win):
        out_shape.append(jax.ShapeDtypeStruct(shape, jnp.bfloat16))
    scratch = [pltpu.VMEM((GROUP * win, 2 * win), jnp.bfloat16)]
    if not with_light:
        out_shape.append(jax.ShapeDtypeStruct((2, win, win), jnp.float32))
        out_shape.append(jax.ShapeDtypeStruct((2, win, win), jnp.bfloat16))
        scratch.append(pltpu.VMEM((GROUP, 2, win, win), jnp.float32))
    return pl.pallas_call(
        functools.partial(sweep_kernel, with_light),
        out_shape=out_shape,
        in_specs=[smem, smem] + [vmem] * 5,
        out_specs=[vmem] * len(out_shape),
        scratch_shapes=scratch,
        compiler_params=pltpu.CompilerParams(vmem_limit_bytes=GRANT),
        name="first_sweep" if with_light else "second_sweep",
    )(corners, live, ext, probe, amp, ahead, back)


MESH = pl.DeviceIdType.MESH


class Place:
    def __init__(self, rows, cols):
        self.row, self.col = lax.axis_index("row"), lax.axis_index("col")
        self.rows, self.cols = rows, cols

    def at(self, down, right):
        return (
            lax.rem(self.row + down + self.rows, self.rows),
            lax.rem(self.col + right + self.cols, self.cols),
        )

    def inside(self, down, right):
        checks = []
        if down:
            checks.append(self.row < self.rows - 1 if down > 0 else self.row > 0)
        if right:
            checks.append(self.col < self.cols - 1 if right > 0 else self.col > 0)
        return checks[0] if len(checks) == 1 else jnp.logical_and(*checks)


def greet(place, steps):
    barrier = pltpu.get_barrier_semaphore()
    for step in steps:

        @pl.when(place.inside(*step))
        def _():
            pl.semaphore_signal(barrier, inc=1, device_id=place.at(*step), device_id_type=MESH)

    return barrier


def meet(place, barrier, steps, others=0):
    for step in steps:
        others = others + jnp.where(place.inside(*step), 1, 0)
    pl.semaphore_wait(barrier, others)


NEAR = ((0, -1), (-1, 0), (-1, -1), (0, 1), (1, 0), (1, 1))


class Shift:
    def __init__(self, place, step, source, target, sems, index):
        self.copy = pltpu.make_async_remote_copy(
            src_ref=source,
            dst_ref=target,
            send_sem=sems.at[0, index],
            recv_sem=sems.at[1, index],
            device_id=place.at(*step),
            device_id_type=MESH,
        )
        self.sends = place.inside(*step)
        self.receives = place.inside(-step[0], -step[1])

    def start(self):
        pl.when(self.sends)(self.copy.start)

    def wait_send(self):
        pl.when(self.sends)(self.copy.wait_send)


def box_shifts(place, down, side, low, corner, sems):
    return [
        Shift(place, (0, down), *side, sems, 0),
        Shift(place, (down, down), *corner, sems, 1),
        Shift(place, (down, 0), *low, sems, 2),
    ]


def finish_sends(shifts):
    for shift in shifts:
        shift.wait_send()


def arrive(shifts, side, low, corner):
    for shift, action in zip((shifts[2], shifts[0], shifts[1]), (low, side, corner)):

        @pl.when(shift.receives)
        def _():
            shift.copy.wait_recv()
            action()


def fill_rims(shifts, ext, side_in, low_in, corner_in):
    win = ext.shape[3]
    tile = ext.shape[2] - win

    def low():
        ext[:, :2, tile:] = low_in[...].astype(jnp.float32)

    def side():
        ext[:, 2, :tile] = side_in[...].astype(jnp.float32)

    def corner():
        ext[:, 2, tile:] = corner_in[...].astype(jnp.float32)

    arrive(shifts, side, low, corner)


def add_spills(shifts, total, side_in, low_in, corner_in):
    win = total.shape[3]

    def low():
        total[:, :, :win] += low_in[...].astype(jnp.float32)

    def side():
        total[:, 0] += side_in[...].astype(jnp.float32)

    def corner():
        total[:, 0, :win] += corner_in[...].astype(jnp.float32)

    arrive(shifts, side, low, corner)


def rim_boxes(place, outs, ins, win, sems):
    side_out, low_out = outs
    side_in, low_in, corner_in = ins
    return box_shifts(
        place,
        -1,
        (side_out, side_in),
        (low_out, low_in),
        (side_out.at[:, pl.ds(0, win)], corner_in),
        sems,
    )


def extend_kernel(rows, cols, obj, ext, side_out, low_out, side_in, low_in, corner_in, sems):
    win = ext.shape[3]
    tile = ext.shape[2] - win
    place = Place(rows, cols)
    barrier = greet(place, NEAR)
    side_out[...] = obj[:, :, :win].astype(jnp.bfloat16)
    for strip in range(2):
        low_out[:, strip] = obj[:, :win, strip * win : (strip + 1) * win].astype(jnp.bfloat16)
    meet(place, barrier, NEAR)
    shifts = rim_boxes(place, (side_out, low_out), (side_in, low_in, corner_in), win, sems)
    for shift in shifts:
        shift.start()
    for strip in range(2):
        ext[:, strip, :tile] = obj[:, :, strip * win : (strip + 1) * win]
    fill_rims(shifts, ext, side_in, low_in, corner_in)
    finish_sends(shifts)


def update_kernel(rows, cols, *refs):
    spread, side_spill, low_spill, corner_spill, obj, ext, inverse = refs[:7]
    side_got, low_got, corner_got, side_out, low_out, side_in, low_in, corner_in = refs[7:15]
    total, sems, rim_sems = refs[15:]
    win = ext.shape[3]
    tile = ext.shape[2] - win
    place = Place(rows, cols)
    barrier = greet(place, NEAR)
    meet(place, barrier, NEAR)
    spills = box_shifts(
        place,
        1,
        (side_spill, side_got),
        (low_spill, low_got),
        (corner_spill, corner_got),
        sems,
    )
    for shift in spills:
        shift.start()
    total[...] = spread[:, :2, :tile]
    add_spills(spills, total, side_got, low_got, corner_got)
    rims = rim_boxes(place, (side_out, low_out), (side_in, low_in, corner_in), win, rim_sems)
    for strip in range(2):
        share = 1.0 / (total[2, strip] + 4.0)
        for plane in range(2):
            fresh = obj[plane, :, strip * win : (strip + 1) * win] + total[plane, strip] * share
            if strip == 0:
                side_out[plane] = fresh.astype(jnp.bfloat16)
            low_out[plane, strip] = fresh[:win].astype(jnp.bfloat16)
            ext[plane, strip, :tile] = fresh
        inverse[strip] = share
        for rim in rims[:2] if strip == 0 else rims[2:]:
            rim.start()
    finish_sends(spills)
    fill_rims(rims, ext, side_in, low_in, corner_in)
    finish_sends(rims)


def last_kernel(rows, cols, *refs):
    spread, side_spill, low_spill, corner_spill, gradient, narrow = refs[:6]
    total, whole, side_got, low_got, corner_got = refs[6:11]
    part_in, peer_in, own, sems, part_sems, peer_sems, whole_sems = refs[11:]
    tile = total.shape[2]
    place = Place(rows, cols)
    diagonal = ((-1, -1), (1, 1))
    barrier = greet(place, diagonal)
    col_peers = [place.at(0, step) for step in range(1, cols)]
    row_peers = [place.at(step, 0) for step in range(1, rows)]
    for peer in col_peers + row_peers:
        pl.semaphore_signal(barrier, inc=1, device_id=peer, device_id_type=MESH)
    meet(place, barrier, diagonal, cols + rows - 2)
    height = whole.shape[0] // rows

    def piece(index):
        return pl.ds(pl.multiple_of(index * height, height), height)

    def send(source, target, pair, index, peer):
        copy = pltpu.make_async_remote_copy(
            src_ref=source,
            dst_ref=target,
            send_sem=pair.at[0, index],
            recv_sem=pair.at[1, index],
            device_id=peer,
            device_id_type=MESH,
        )
        copy.start()
        return copy

    parts = [
        send(narrow.at[piece(peer[0])], part_in.at[index], part_sems, index, peer)
        for index, peer in enumerate(row_peers)
    ]
    spills = box_shifts(
        place,
        1,
        (side_spill, side_got),
        (low_spill, low_got),
        (corner_spill, corner_got),
        sems,
    )
    for shift in spills:
        shift.start()
    summed = gradient[piece(place.row)]
    for index, copy in enumerate(parts):
        copy.wait_recv()
        summed = summed + part_in[index].astype(jnp.float32)
    own[...] = summed.astype(jnp.bfloat16)
    peer_in[place.col] = summed.astype(jnp.bfloat16)
    peers = [
        send(own, peer_in.at[place.col], peer_sems, index, peer)
        for index, peer in enumerate(col_peers)
    ]
    total[...] = spread[:, :2, :tile]
    for copy in peers:
        copy.wait_recv()
    summed = peer_in[0].astype(jnp.float32)
    for index in range(1, cols):
        summed = summed + peer_in[index].astype(jnp.float32)
    whole[piece(place.row)] = summed
    gathers = [
        send(whole.at[piece(place.row)], whole.at[piece(place.row)], whole_sems, index, peer)
        for index, peer in enumerate(row_peers)
    ]
    add_spills(spills, total, side_got, low_got, corner_got)
    for copy in gathers:
        copy.wait_recv()
    for copy in parts + peers + gathers:
        copy.wait_send()
    finish_sends(spills)


def close_kernel(ext, total, inverse, whole, probe, refined, new_probe):
    win = ext.shape[3]
    tile = ext.shape[2] - win
    for strip in range(2):
        for plane in range(2):
            refined[plane, :, strip * win : (strip + 1) * win] = (
                ext[plane, strip, :tile] + total[plane, strip] * inverse[strip]
            )
    value = whole[...]
    power = jnp.sum(value * value, axis=(0, 1), keepdims=True) / (value.shape[0] // 2 * win)
    new_probe[...] = probe[...] + value * lax.rsqrt(power + 1e-06)


def remote_call(kernel, ident, out_shape, scratch, operands):
    vmem = pl.BlockSpec(memory_space=pltpu.VMEM)
    return pl.pallas_call(
        kernel,
        out_shape=out_shape,
        in_specs=[vmem] * len(operands),
        out_specs=[vmem] * len(out_shape),
        scratch_shapes=scratch,
        compiler_params=pltpu.CompilerParams(
            collective_id=ident, has_side_effects=True, vmem_limit_bytes=GRANT
        ),
    )(*operands)


def on_device(rows, cols, object_field, probe, amplitude, corners, live_count):
    slots = amplitude.shape[2]
    win = probe.shape[1]
    tile = object_field.shape[1]
    amp = amplitude.reshape(slots, win, win)
    corners = corners.reshape(2, slots)
    live = live_count.reshape(1)
    ahead, back = dft_tables(win)
    f32, b16 = jnp.float32, jnp.bfloat16
    sem = pltpu.SemaphoreType.DMA
    ext_shape = jax.ShapeDtypeStruct((2, tile // win + 1, tile + win, win), f32)

    def boxes(planes, count=3):
        return [pltpu.VMEM(shape, b16) for shape in spill_shapes(planes, tile, win)[:count]]

    (ext,) = remote_call(
        functools.partial(extend_kernel, rows, cols),
        0,
        [ext_shape],
        boxes(2, 2) + boxes(2) + [sem((2, 3))],
        [object_field],
    )
    spread, *spills = sweep(True, corners, live, ext, probe, amp, ahead, back)
    ext, inverse = remote_call(
        functools.partial(update_kernel, rows, cols),
        1,
        [ext_shape, jax.ShapeDtypeStruct((2, tile, win), f32)],
        boxes(3)
        + boxes(2, 2)
        + boxes(2)
        + [pltpu.VMEM((3, 2, tile, win), f32), sem((2, 3)), sem((2, 3))],
        [spread, *spills, object_field],
    )
    spread, *spills, gradient, narrow = sweep(False, corners, live, ext, probe, amp, ahead, back)
    flat = (2 * win, win)
    height = 2 * win // rows
    total, whole = remote_call(
        functools.partial(last_kernel, rows, cols),
        2,
        [jax.ShapeDtypeStruct((2, 2, tile, win), f32), jax.ShapeDtypeStruct(flat, f32)],
        boxes(2)
        + [
            pltpu.VMEM((rows - 1, height, win), b16),
            pltpu.VMEM((cols, height, win), b16),
            pltpu.VMEM((height, win), b16),
            sem((2, 3)),
            sem((2, rows - 1)),
            sem((2, cols - 1)),
            sem((2, rows - 1)),
        ],
        [spread, *spills, gradient.reshape(flat), narrow.reshape(flat)],
    )
    vmem = pl.BlockSpec(memory_space=pltpu.VMEM)
    refined, new_probe = pl.pallas_call(
        close_kernel,
        out_shape=[jax.ShapeDtypeStruct(object_field.shape, f32), jax.ShapeDtypeStruct(flat, f32)],
        in_specs=[vmem] * 5,
        out_specs=[vmem] * 2,
        compiler_params=pltpu.CompilerParams(vmem_limit_bytes=GRANT),
        name="close",
    )(ext, total, inverse, whole, probe.reshape(flat))
    return (refined, new_probe.reshape(probe.shape))


def solution(mesh):
    in_specs = (
        P(None, "row", "col"),
        P(),
        P("row", "col", None, None, None),
        P(None, "row", "col", None),
        P("row", "col"),
    )
    out_specs = (P(None, "row", "col"), P())
    return jax.shard_map(
        functools.partial(on_device, mesh.shape["row"], mesh.shape["col"]), mesh=mesh, in_specs=in_specs, out_specs=out_specs, check_vma=False
    )
```

```python
import functools
import math

import jax
import jax.numpy as jnp
import numpy as np
from jax import lax
from jax.experimental import pallas as pl
from jax.experimental.pallas import tpu as pltpu
from jax.sharding import PartitionSpec as P

GROUP = 8
GRANT = 12 << 20


def dft_tables(window):
    indices = np.arange(window, dtype=np.int32)
    phase_index = indices[:, None] * indices[None, :] % window
    angles = phase_index.astype(np.float32) * np.float32(2.0 * math.pi / window)
    norming = np.float32(1.0 / math.sqrt(window))
    cosines = np.cos(angles) * norming
    sines = np.sin(angles) * norming
    forward = np.block([[cosines, -sines], [sines, cosines]]).astype(np.float32)
    return (jnp.asarray(forward, jnp.bfloat16), jnp.asarray(forward.T.copy(), jnp.bfloat16))


def dot(left, right):
    return jnp.dot(left, right, preferred_element_type=jnp.float32)


def sweep_kernel(with_light, corners, live, ext, probe, amp, ahead, back, deposit, *rest):
    side_out, low_out, corner_out = rest[:3]
    if with_light:
        waves_buf = rest[3]
    else:
        gradient, narrow, waves_buf, patch_buf = rest[3:]
        gradient[...] = jnp.zeros_like(gradient)
    slots, win = amp.shape[0], amp.shape[1]
    deposit[...] = jnp.zeros_like(deposit)
    lane = lax.broadcasted_iota(jnp.int32, (win, win), 1)
    used = live[0]

    def spot(slot):
        row, col = corners[0, slot], corners[1, slot]
        base = col // win
        return row, base, col - base * win

    def add_at(plane, row, base, shift, value):
        turned = pltpu.roll(value, shift, 1)
        left = jnp.where(lane >= shift, turned, 0.0)
        right = jnp.where(lane >= shift, 0.0, turned)
        for offset, part in ((0, left), (1, right)):
            at = (plane, base + offset, pl.ds(row, win))
            deposit[at] = deposit[at] + part

    @pl.loop(0, (used + GROUP - 1) // GROUP)
    def _(turn):
        first = turn * GROUP
        pr, pi = probe[0], probe[1]
        for member in range(GROUP):
            row, base, shift = spot(first + member)
            parts = []
            for plane in range(2):
                left = ext[plane, base, pl.ds(row, win)]
                right = ext[plane, base + 1, pl.ds(row, win)]
                mixed = jnp.where(lane >= shift, left, right)
                parts.append(pltpu.roll(mixed, lax.rem(win - shift, win), 1))
            re, im = parts
            if not with_light:
                patch_buf[member, 0] = re
                patch_buf[member, 1] = im
            rows = pl.ds(member * win, win)
            waves_buf[rows, :win] = (pr * re - pi * im).astype(jnp.bfloat16)
            waves_buf[rows, win:] = (pr * im + pi * re).astype(jnp.bfloat16)
        half = dot(waves_buf[...], ahead[...]).astype(jnp.bfloat16)

        def upright(value):
            columns = []
            for member in range(GROUP):
                block = value[member * win : (member + 1) * win]
                columns.append(jnp.concatenate([block[:, :win], block[:, win:]], 0))
            return jnp.concatenate(columns, 1)

        spectrum = dot(back[...], upright(half))
        projected = []
        for member in range(GROUP):
            re = spectrum[:win, member * win : (member + 1) * win]
            im = spectrum[win:, member * win : (member + 1) * win]
            scale = amp[first + member].astype(jnp.float32) * lax.rsqrt(
                jnp.maximum(re * re + im * im, 0.25)
            )
            projected.append(
                jnp.concatenate(
                    [(re * scale).astype(jnp.bfloat16), (im * scale).astype(jnp.bfloat16)], 1
                )
            )
        half_back = dot(jnp.concatenate(projected, 0), back[...]).astype(jnp.bfloat16)
        returned = dot(ahead[...], upright(half_back))
        for member in range(GROUP):
            slot = first + member
            weight = jnp.where(slot < used, 1.0, 0.0)
            row, base, shift = spot(slot)
            rows = pl.ds(member * win, win)
            columns = slice(member * win, (member + 1) * win)
            re = (returned[:win, columns] - waves_buf[rows, :win].astype(jnp.float32)) * weight
            im = (returned[win:, columns] - waves_buf[rows, win:].astype(jnp.float32)) * weight
            add_at(0, row, base, shift, pr * re + pi * im)
            add_at(1, row, base, shift, pr * im - pi * re)
            if with_light:
                add_at(2, row, base, shift, (pr * pr + pi * pi) * weight)
            else:
                ore, oim = patch_buf[member, 0], patch_buf[member, 1]
                gradient[0] += ore * re + oim * im
                gradient[1] += ore * im - oim * re

    tile = deposit.shape[2] - win
    side_out[...] = deposit[:, 2, :tile].astype(jnp.bfloat16)
    low_out[...] = deposit[:, :2, tile:].astype(jnp.bfloat16)
    corner_out[...] = deposit[:, 2, tile:].astype(jnp.bfloat16)
    if not with_light:
        narrow[...] = gradient[...].astype(jnp.bfloat16)


def spill_shapes(planes, tile, win):
    return [(planes, tile, win), (planes, 2, win, win), (planes, win, win)]


def sweep(with_light, corners, live, ext, probe, amp, ahead, back):
    slots, win = amp.shape[0], amp.shape[1]
    strips, side = ext.shape[1:3]
    vmem = pl.BlockSpec(memory_space=pltpu.VMEM)
    smem = pl.BlockSpec(memory_space=pltpu.SMEM)
    planes = 3 if with_light else 2
    out_shape = [jax.ShapeDtypeStruct((planes, strips, side, win), jnp.float32)]
    for shape in spill_shapes(planes, side - win, win):
        out_shape.append(jax.ShapeDtypeStruct(shape, jnp.bfloat16))
    scratch = [pltpu.VMEM((GROUP * win, 2 * win), jnp.bfloat16)]
    if not with_light:
        out_shape.append(jax.ShapeDtypeStruct((2, win, win), jnp.float32))
        out_shape.append(jax.ShapeDtypeStruct((2, win, win), jnp.bfloat16))
        scratch.append(pltpu.VMEM((GROUP, 2, win, win), jnp.float32))
    return pl.pallas_call(
        functools.partial(sweep_kernel, with_light),
        out_shape=out_shape,
        in_specs=[smem, smem] + [vmem] * 5,
        out_specs=[vmem] * len(out_shape),
        scratch_shapes=scratch,
        compiler_params=pltpu.CompilerParams(vmem_limit_bytes=GRANT),
        name="first_sweep" if with_light else "second_sweep",
    )(corners, live, ext, probe, amp, ahead, back)


MESH = pl.DeviceIdType.MESH


class Place:
    def __init__(self, rows, cols):
        self.row, self.col = lax.axis_index("row"), lax.axis_index("col")
        self.rows, self.cols = rows, cols

    def at(self, down, right):
        return (
            lax.rem(self.row + down + self.rows, self.rows),
            lax.rem(self.col + right + self.cols, self.cols),
        )

    def inside(self, down, right):
        checks = []
        if down:
            checks.append(self.row < self.rows - 1 if down > 0 else self.row > 0)
        if right:
            checks.append(self.col < self.cols - 1 if right > 0 else self.col > 0)
        return checks[0] if len(checks) == 1 else jnp.logical_and(*checks)


def greet(place, steps):
    barrier = pltpu.get_barrier_semaphore()
    for step in steps:

        @pl.when(place.inside(*step))
        def _():
            pl.semaphore_signal(barrier, inc=1, device_id=place.at(*step), device_id_type=MESH)

    return barrier


def meet(place, barrier, steps, others=0):
    for step in steps:
        others = others + jnp.where(place.inside(*step), 1, 0)
    pl.semaphore_wait(barrier, others)


NEXT = ((0, -1), (-1, 0), (0, 1), (1, 0))
NEAR = ((0, -1), (-1, 0), (-1, -1), (0, 1), (1, 0), (1, 1))


class Shift:
    def __init__(self, place, step, source, target, sems, index):
        self.copy = pltpu.make_async_remote_copy(
            src_ref=source,
            dst_ref=target,
            send_sem=sems.at[0, index],
            recv_sem=sems.at[1, index],
            device_id=place.at(*step),
            device_id_type=MESH,
        )
        self.sends = place.inside(*step)
        self.receives = place.inside(-step[0], -step[1])

    def start(self):
        pl.when(self.sends)(self.copy.start)

    def wait_send(self):
        pl.when(self.sends)(self.copy.wait_send)


def box_shifts(place, down, side, low, corner, sems):
    return [
        Shift(place, (0, down), *side, sems, 0),
        Shift(place, (down, down), *corner, sems, 1),
        Shift(place, (down, 0), *low, sems, 2),
    ]


def finish_sends(shifts):
    for shift in shifts:
        shift.wait_send()


def arrive(shifts, side, low, corner):
    for shift, action in zip((shifts[2], shifts[0], shifts[1]), (low, side, corner)):

        @pl.when(shift.receives)
        def _():
            shift.copy.wait_recv()
            action()


def fill_rims(shifts, ext, side_in, low_in, corner_in):
    win = ext.shape[3]
    tile = ext.shape[2] - win
    top, bottom, low, onward = shifts

    @pl.when(top.receives)
    def _():
        top.copy.wait_recv()

    onward.start()

    @pl.when(low.receives)
    def _():
        low.copy.wait_recv()
        ext[:, :2, tile:] = low_in[...].astype(jnp.float32)

    @pl.when(bottom.receives)
    def _():
        bottom.copy.wait_recv()
        ext[:, 2, :tile] = side_in[...].astype(jnp.float32)

    @pl.when(onward.receives)
    def _():
        onward.copy.wait_recv()
        ext[:, 2, tile:] = corner_in[...].astype(jnp.float32)


def add_spills(shifts, total, side_in, low_in, corner_in):
    win = total.shape[3]

    def low():
        total[:, :, :win] += low_in[...].astype(jnp.float32)

    def side():
        total[:, 0] += side_in[...].astype(jnp.float32)

    def corner():
        total[:, 0, :win] += corner_in[...].astype(jnp.float32)

    arrive(shifts, side, low, corner)


def rim_boxes(place, outs, ins, win, sems):
    side_out, low_out = outs
    side_in, low_in, corner_in = ins
    top, bottom = pl.ds(0, win), pl.ds(win, side_in.shape[1] - win)
    left = (0, -1)
    onward = Shift(place, (-1, 0), side_in.at[:, top], corner_in, sems, 3)
    onward.sends = place.inside(-1, 1)
    onward.receives = place.inside(1, 1)
    return [
        Shift(place, left, side_out.at[:, top], side_in.at[:, top], sems, 0),
        Shift(place, left, side_out.at[:, bottom], side_in.at[:, bottom], sems, 1),
        Shift(place, (-1, 0), low_out, low_in, sems, 2),
        onward,
    ]


def extend_kernel(rows, cols, obj, ext, side_out, low_out, side_in, low_in, corner_in, sems):
    win = ext.shape[3]
    tile = ext.shape[2] - win
    place = Place(rows, cols)
    barrier = greet(place, NEXT)
    side_out[...] = obj[:, :, :win].astype(jnp.bfloat16)
    for strip in range(2):
        low_out[:, strip] = obj[:, :win, strip * win : (strip + 1) * win].astype(jnp.bfloat16)
    meet(place, barrier, NEXT)
    shifts = rim_boxes(place, (side_out, low_out), (side_in, low_in, corner_in), win, sems)
    for shift in shifts[:3]:
        shift.start()
    for strip in range(2):
        ext[:, strip, :tile] = obj[:, :, strip * win : (strip + 1) * win]
    fill_rims(shifts, ext, side_in, low_in, corner_in)
    finish_sends(shifts)


def update_kernel(rows, cols, *refs):
    spread, side_spill, low_spill, corner_spill, obj, ext, inverse = refs[:7]
    side_got, low_got, corner_got, side_out, low_out, side_in, low_in, corner_in = refs[7:15]
    total, sems, rim_sems = refs[15:]
    win = ext.shape[3]
    tile = ext.shape[2] - win
    place = Place(rows, cols)
    barrier = greet(place, NEAR)
    meet(place, barrier, NEAR)
    spills = box_shifts(
        place,
        1,
        (side_spill, side_got),
        (low_spill, low_got),
        (corner_spill, corner_got),
        sems,
    )
    for shift in spills:
        shift.start()
    total[...] = spread[:, :2, :tile]
    add_spills(spills, total, side_got, low_got, corner_got)
    rims = rim_boxes(place, (side_out, low_out), (side_in, low_in, corner_in), win, rim_sems)
    for strip in range(2):
        share = 1.0 / (total[2, strip] + 4.0)
        for plane in range(2):
            fresh = obj[plane, :, strip * win : (strip + 1) * win] + total[plane, strip] * share
            if strip == 0:
                side_out[plane] = fresh.astype(jnp.bfloat16)
            low_out[plane, strip] = fresh[:win].astype(jnp.bfloat16)
            ext[plane, strip, :tile] = fresh
        inverse[strip] = share
        for rim in rims[:2] if strip == 0 else rims[2:3]:
            rim.start()
    finish_sends(spills)
    fill_rims(rims, ext, side_in, low_in, corner_in)
    finish_sends(rims)


def last_kernel(rows, cols, *refs):
    spread, side_spill, low_spill, corner_spill, gradient, narrow = refs[:6]
    total, whole, side_got, low_got, corner_got = refs[6:11]
    part_in, peer_in, own, sems, part_sems, peer_sems, whole_sems = refs[11:]
    tile = total.shape[2]
    place = Place(rows, cols)
    diagonal = ((-1, -1), (1, 1))
    barrier = greet(place, diagonal)
    col_peers = [place.at(0, step) for step in range(1, cols)]
    row_peers = [place.at(step, 0) for step in range(1, rows)]
    for peer in col_peers + row_peers:
        pl.semaphore_signal(barrier, inc=1, device_id=peer, device_id_type=MESH)
    meet(place, barrier, diagonal, cols + rows - 2)
    height = whole.shape[0] // rows

    def piece(index):
        return pl.ds(pl.multiple_of(index * height, height), height)

    def send(source, target, pair, index, peer):
        copy = pltpu.make_async_remote_copy(
            src_ref=source,
            dst_ref=target,
            send_sem=pair.at[0, index],
            recv_sem=pair.at[1, index],
            device_id=peer,
            device_id_type=MESH,
        )
        copy.start()
        return copy

    parts = [
        send(narrow.at[piece(peer[0])], part_in.at[index], part_sems, index, peer)
        for index, peer in enumerate(row_peers)
    ]
    spills = box_shifts(
        place,
        1,
        (side_spill, side_got),
        (low_spill, low_got),
        (corner_spill, corner_got),
        sems,
    )
    for shift in spills:
        shift.start()
    summed = gradient[piece(place.row)]
    for index, copy in enumerate(parts):
        copy.wait_recv()
        summed = summed + part_in[index].astype(jnp.float32)
    own[...] = summed.astype(jnp.bfloat16)
    peer_in[place.col] = summed.astype(jnp.bfloat16)
    peers = [
        send(own, peer_in.at[place.col], peer_sems, index, peer)
        for index, peer in enumerate(col_peers)
    ]
    total[...] = spread[:, :2, :tile]
    for copy in peers:
        copy.wait_recv()
    summed = peer_in[0].astype(jnp.float32)
    for index in range(1, cols):
        summed = summed + peer_in[index].astype(jnp.float32)
    whole[piece(place.row)] = summed
    gathers = [
        send(whole.at[piece(place.row)], whole.at[piece(place.row)], whole_sems, index, peer)
        for index, peer in enumerate(row_peers)
    ]
    add_spills(spills, total, side_got, low_got, corner_got)
    for copy in gathers:
        copy.wait_recv()
    for copy in parts + peers + gathers:
        copy.wait_send()
    finish_sends(spills)


def close_kernel(ext, total, inverse, whole, probe, refined, new_probe):
    win = ext.shape[3]
    tile = ext.shape[2] - win
    for strip in range(2):
        for plane in range(2):
            refined[plane, :, strip * win : (strip + 1) * win] = (
                ext[plane, strip, :tile] + total[plane, strip] * inverse[strip]
            )
    value = whole[...]
    power = jnp.sum(value * value, axis=(0, 1), keepdims=True) / (value.shape[0] // 2 * win)
    new_probe[...] = probe[...] + value * lax.rsqrt(power + 1e-06)


def remote_call(kernel, ident, out_shape, scratch, operands):
    vmem = pl.BlockSpec(memory_space=pltpu.VMEM)
    return pl.pallas_call(
        kernel,
        out_shape=out_shape,
        in_specs=[vmem] * len(operands),
        out_specs=[vmem] * len(out_shape),
        scratch_shapes=scratch,
        compiler_params=pltpu.CompilerParams(
            collective_id=ident, has_side_effects=True, vmem_limit_bytes=GRANT
        ),
    )(*operands)


def on_device(rows, cols, object_field, probe, amplitude, corners, live_count):
    slots = amplitude.shape[2]
    win = probe.shape[1]
    tile = object_field.shape[1]
    amp = amplitude.reshape(slots, win, win)
    corners = corners.reshape(2, slots)
    live = live_count.reshape(1)
    ahead, back = dft_tables(win)
    f32, b16 = jnp.float32, jnp.bfloat16
    sem = pltpu.SemaphoreType.DMA
    ext_shape = jax.ShapeDtypeStruct((2, tile // win + 1, tile + win, win), f32)

    def boxes(planes, count=3):
        return [pltpu.VMEM(shape, b16) for shape in spill_shapes(planes, tile, win)[:count]]

    (ext,) = remote_call(
        functools.partial(extend_kernel, rows, cols),
        0,
        [ext_shape],
        boxes(2, 2) + boxes(2) + [sem((2, 4))],
        [object_field],
    )
    spread, *spills = sweep(True, corners, live, ext, probe, amp, ahead, back)
    ext, inverse = remote_call(
        functools.partial(update_kernel, rows, cols),
        1,
        [ext_shape, jax.ShapeDtypeStruct((2, tile, win), f32)],
        boxes(3)
        + boxes(2, 2)
        + boxes(2)
        + [pltpu.VMEM((3, 2, tile, win), f32), sem((2, 3)), sem((2, 4))],
        [spread, *spills, object_field],
    )
    spread, *spills, gradient, narrow = sweep(False, corners, live, ext, probe, amp, ahead, back)
    flat = (2 * win, win)
    height = 2 * win // rows
    total, whole = remote_call(
        functools.partial(last_kernel, rows, cols),
        2,
        [jax.ShapeDtypeStruct((2, 2, tile, win), f32), jax.ShapeDtypeStruct(flat, f32)],
        boxes(2)
        + [
            pltpu.VMEM((rows - 1, height, win), b16),
            pltpu.VMEM((cols, height, win), b16),
            pltpu.VMEM((height, win), b16),
            sem((2, 3)),
            sem((2, rows - 1)),
            sem((2, cols - 1)),
            sem((2, rows - 1)),
        ],
        [spread, *spills, gradient.reshape(flat), narrow.reshape(flat)],
    )
    vmem = pl.BlockSpec(memory_space=pltpu.VMEM)
    refined, new_probe = pl.pallas_call(
        close_kernel,
        out_shape=[jax.ShapeDtypeStruct(object_field.shape, f32), jax.ShapeDtypeStruct(flat, f32)],
        in_specs=[vmem] * 5,
        out_specs=[vmem] * 2,
        compiler_params=pltpu.CompilerParams(vmem_limit_bytes=GRANT),
        name="close",
    )(ext, total, inverse, whole, probe.reshape(flat))
    return (refined, new_probe.reshape(probe.shape))


def solution(mesh):
    in_specs = (
        P(None, "row", "col"),
        P(),
        P("row", "col", None, None, None),
        P(None, "row", "col", None),
        P("row", "col"),
    )
    out_specs = (P(None, "row", "col"), P())
    return jax.shard_map(
        functools.partial(on_device, mesh.shape["row"], mesh.shape["col"]), mesh=mesh, in_specs=in_specs, out_specs=out_specs, check_vma=False
    )
```

```python
import functools
import math

import jax
import jax.numpy as jnp
import numpy as np
from jax import lax
from jax.experimental import pallas as pl
from jax.experimental.pallas import tpu as pltpu
from jax.sharding import PartitionSpec as P

GROUP = 8
GRANT = 12 << 20


def dft_tables(window):
    indices = np.arange(window, dtype=np.int32)
    phase_index = indices[:, None] * indices[None, :] % window
    angles = phase_index.astype(np.float32) * np.float32(2.0 * math.pi / window)
    norming = np.float32(1.0 / math.sqrt(window))
    cosines = np.cos(angles) * norming
    sines = np.sin(angles) * norming
    forward = np.block([[cosines, -sines], [sines, cosines]]).astype(np.float32)
    return (jnp.asarray(forward, jnp.bfloat16), jnp.asarray(forward.T.copy(), jnp.bfloat16))


def dot(left, right):
    return jnp.dot(left, right, preferred_element_type=jnp.float32)


def sweep_kernel(with_light, corners, live, ext, probe, amp, ahead, back, deposit, *rest):
    side_out, low_out, corner_out = rest[:3]
    if with_light:
        waves_buf = rest[3]
    else:
        gradient, narrow, waves_buf, patch_buf = rest[3:]
        gradient[...] = jnp.zeros_like(gradient)
    slots, win = amp.shape[0], amp.shape[1]
    deposit[...] = jnp.zeros_like(deposit)
    lane = lax.broadcasted_iota(jnp.int32, (win, win), 1)
    used = live[0]

    def spot(slot):
        row, col = corners[0, slot], corners[1, slot]
        base = col // win
        return row, base, col - base * win

    def add_at(plane, row, base, shift, value):
        turned = pltpu.roll(value, shift, 1)
        left = jnp.where(lane >= shift, turned, 0.0)
        right = jnp.where(lane >= shift, 0.0, turned)
        for offset, part in ((0, left), (1, right)):
            at = (plane, base + offset, pl.ds(row, win))
            deposit[at] = deposit[at] + part

    @pl.loop(0, (used + GROUP - 1) // GROUP)
    def _(turn):
        first = turn * GROUP
        pr, pi = probe[0], probe[1]
        for member in range(GROUP):
            row, base, shift = spot(first + member)
            parts = []
            for plane in range(2):
                left = ext[plane, base, pl.ds(row, win)]
                right = ext[plane, base + 1, pl.ds(row, win)]
                mixed = jnp.where(lane >= shift, left, right)
                parts.append(pltpu.roll(mixed, lax.rem(win - shift, win), 1))
            re, im = parts
            if not with_light:
                patch_buf[member, 0] = re
                patch_buf[member, 1] = im
            rows = pl.ds(member * win, win)
            waves_buf[rows, :win] = (pr * re - pi * im).astype(jnp.bfloat16)
            waves_buf[rows, win:] = (pr * im + pi * re).astype(jnp.bfloat16)
        half = dot(waves_buf[...], ahead[...]).astype(jnp.bfloat16)

        def upright(value):
            columns = []
            for member in range(GROUP):
                block = value[member * win : (member + 1) * win]
                columns.append(jnp.concatenate([block[:, :win], block[:, win:]], 0))
            return jnp.concatenate(columns, 1)

        spectrum = dot(back[...], upright(half))
        projected = []
        for member in range(GROUP):
            re = spectrum[:win, member * win : (member + 1) * win]
            im = spectrum[win:, member * win : (member + 1) * win]
            scale = amp[first + member].astype(jnp.float32) * lax.rsqrt(
                jnp.maximum(re * re + im * im, 0.25)
            )
            projected.append(
                jnp.concatenate(
                    [(re * scale).astype(jnp.bfloat16), (im * scale).astype(jnp.bfloat16)], 1
                )
            )
        half_back = dot(jnp.concatenate(projected, 0), back[...]).astype(jnp.bfloat16)
        returned = dot(ahead[...], upright(half_back))
        for member in range(GROUP):
            slot = first + member
            weight = jnp.where(slot < used, 1.0, 0.0)
            row, base, shift = spot(slot)
            rows = pl.ds(member * win, win)
            columns = slice(member * win, (member + 1) * win)
            re = (returned[:win, columns] - waves_buf[rows, :win].astype(jnp.float32)) * weight
            im = (returned[win:, columns] - waves_buf[rows, win:].astype(jnp.float32)) * weight
            add_at(0, row, base, shift, pr * re + pi * im)
            add_at(1, row, base, shift, pr * im - pi * re)
            if with_light:
                add_at(2, row, base, shift, (pr * pr + pi * pi) * weight)
            else:
                ore, oim = patch_buf[member, 0], patch_buf[member, 1]
                gradient[0] += ore * re + oim * im
                gradient[1] += ore * im - oim * re

    tile = deposit.shape[2] - win
    side_out[...] = deposit[:, 2, :tile].astype(jnp.bfloat16)
    low_out[...] = deposit[:, :2, tile:].astype(jnp.bfloat16)
    corner_out[...] = deposit[:, 2, tile:].astype(jnp.bfloat16)
    if not with_light:
        narrow[...] = gradient[...].astype(jnp.bfloat16)


def spill_shapes(planes, tile, win):
    return [(planes, tile, win), (planes, 2, win, win), (planes, win, win)]


def sweep(with_light, corners, live, ext, probe, amp, ahead, back):
    slots, win = amp.shape[0], amp.shape[1]
    strips, side = ext.shape[1:3]
    vmem = pl.BlockSpec(memory_space=pltpu.VMEM)
    smem = pl.BlockSpec(memory_space=pltpu.SMEM)
    planes = 3 if with_light else 2
    out_shape = [jax.ShapeDtypeStruct((planes, strips, side, win), jnp.float32)]
    for shape in spill_shapes(planes, side - win, win):
        out_shape.append(jax.ShapeDtypeStruct(shape, jnp.bfloat16))
    scratch = [pltpu.VMEM((GROUP * win, 2 * win), jnp.bfloat16)]
    if not with_light:
        out_shape.append(jax.ShapeDtypeStruct((2, win, win), jnp.float32))
        out_shape.append(jax.ShapeDtypeStruct((2, win, win), jnp.bfloat16))
        scratch.append(pltpu.VMEM((GROUP, 2, win, win), jnp.float32))
    return pl.pallas_call(
        functools.partial(sweep_kernel, with_light),
        out_shape=out_shape,
        in_specs=[smem, smem] + [vmem] * 5,
        out_specs=[vmem] * len(out_shape),
        scratch_shapes=scratch,
        compiler_params=pltpu.CompilerParams(vmem_limit_bytes=GRANT),
        name="first_sweep" if with_light else "second_sweep",
    )(corners, live, ext, probe, amp, ahead, back)


MESH = pl.DeviceIdType.MESH


class Place:
    def __init__(self, rows, cols):
        self.row, self.col = lax.axis_index("row"), lax.axis_index("col")
        self.rows, self.cols = rows, cols

    def at(self, down, right):
        return (
            lax.rem(self.row + down + self.rows, self.rows),
            lax.rem(self.col + right + self.cols, self.cols),
        )

    def inside(self, down, right):
        checks = []
        if down:
            checks.append(self.row < self.rows - 1 if down > 0 else self.row > 0)
        if right:
            checks.append(self.col < self.cols - 1 if right > 0 else self.col > 0)
        return checks[0] if len(checks) == 1 else jnp.logical_and(*checks)


def greet(place, steps):
    barrier = pltpu.get_barrier_semaphore()
    for step in steps:

        @pl.when(place.inside(*step))
        def _():
            pl.semaphore_signal(barrier, inc=1, device_id=place.at(*step), device_id_type=MESH)

    return barrier


def meet(place, barrier, steps, others=0):
    for step in steps:
        others = others + jnp.where(place.inside(*step), 1, 0)
    pl.semaphore_wait(barrier, others)


NEXT = ((0, -1), (-1, 0), (0, 1), (1, 0))


class Shift:
    def __init__(self, place, step, source, target, sems, index):
        self.copy = pltpu.make_async_remote_copy(
            src_ref=source,
            dst_ref=target,
            send_sem=sems.at[0, index],
            recv_sem=sems.at[1, index],
            device_id=place.at(*step),
            device_id_type=MESH,
        )
        self.sends = place.inside(*step)
        self.receives = place.inside(-step[0], -step[1])

    def start(self):
        pl.when(self.sends)(self.copy.start)

    def wait_send(self):
        pl.when(self.sends)(self.copy.wait_send)


def spill_shifts(place, spills, got, mixed, sems):
    side, low, corner = spills
    side_got, low_got, corner_got = got
    win = corner.shape[1]
    top, bottom = pl.ds(0, win), pl.ds(win, side.shape[1] - win)
    below = Shift(place, (1, 0), corner, corner_got, sems, 0)
    below.sends = place.inside(1, 1)
    below.receives = place.inside(-1, 1)
    return [
        below,
        Shift(place, (0, 1), side.at[:, bottom], side_got.at[:, bottom], sems, 1),
        Shift(place, (1, 0), low, low_got, sems, 2),
        Shift(place, (0, 1), mixed, side_got.at[:, top], sems, 3),
    ]


def pass_corner(shifts, spread, side, corner_got, mixed):
    win = corner_got.shape[1]
    below = shifts[0]

    @pl.when(below.receives)
    def _():
        below.copy.wait_recv()
        mixed[...] = (spread[:, 2, :win] + corner_got[...].astype(jnp.float32)).astype(jnp.bfloat16)

    @pl.when(jnp.logical_not(below.receives))
    def _():
        mixed[...] = side[:, :win]

    shifts[3].start()


def finish_sends(shifts):
    for shift in shifts:
        shift.wait_send()


def fill_rims(shifts, ext, side_in, low_in, corner_in):
    win = ext.shape[3]
    tile = ext.shape[2] - win
    top, bottom, low, onward = shifts

    @pl.when(top.receives)
    def _():
        top.copy.wait_recv()

    onward.start()

    @pl.when(low.receives)
    def _():
        low.copy.wait_recv()
        ext[:, :2, tile:] = low_in[...].astype(jnp.float32)

    @pl.when(bottom.receives)
    def _():
        bottom.copy.wait_recv()
        ext[:, 2, :tile] = side_in[...].astype(jnp.float32)

    @pl.when(onward.receives)
    def _():
        onward.copy.wait_recv()
        ext[:, 2, tile:] = corner_in[...].astype(jnp.float32)


def add_spills(shifts, total, got):
    side_got, low_got, corner_got = got
    win = total.shape[3]
    below, bottom, low, top = shifts

    @pl.when(low.receives)
    def _():
        low.copy.wait_recv()
        total[:, :, :win] += low_got[...].astype(jnp.float32)

    @pl.when(bottom.receives)
    def _():
        bottom.copy.wait_recv()
        total[:, 0, win:] += side_got[:, win:].astype(jnp.float32)

    @pl.when(top.receives)
    def _():
        top.copy.wait_recv()
        total[:, 0, :win] += side_got[:, :win].astype(jnp.float32)


def rim_boxes(place, outs, ins, win, sems):
    side_out, low_out = outs
    side_in, low_in, corner_in = ins
    top, bottom = pl.ds(0, win), pl.ds(win, side_in.shape[1] - win)
    left = (0, -1)
    onward = Shift(place, (-1, 0), side_in.at[:, top], corner_in, sems, 3)
    onward.sends = place.inside(-1, 1)
    onward.receives = place.inside(1, 1)
    return [
        Shift(place, left, side_out.at[:, top], side_in.at[:, top], sems, 0),
        Shift(place, left, side_out.at[:, bottom], side_in.at[:, bottom], sems, 1),
        Shift(place, (-1, 0), low_out, low_in, sems, 2),
        onward,
    ]


def extend_kernel(rows, cols, obj, ext, side_out, low_out, side_in, low_in, corner_in, sems):
    win = ext.shape[3]
    tile = ext.shape[2] - win
    place = Place(rows, cols)
    barrier = greet(place, NEXT)
    side_out[...] = obj[:, :, :win].astype(jnp.bfloat16)
    for strip in range(2):
        low_out[:, strip] = obj[:, :win, strip * win : (strip + 1) * win].astype(jnp.bfloat16)
    meet(place, barrier, NEXT)
    shifts = rim_boxes(place, (side_out, low_out), (side_in, low_in, corner_in), win, sems)
    for shift in shifts[:3]:
        shift.start()
    for strip in range(2):
        ext[:, strip, :tile] = obj[:, :, strip * win : (strip + 1) * win]
    fill_rims(shifts, ext, side_in, low_in, corner_in)
    finish_sends(shifts)


def update_kernel(rows, cols, *refs):
    spread, side_spill, low_spill, corner_spill, obj, ext, inverse = refs[:7]
    got = refs[7:10]
    side_out, low_out, side_in, low_in, corner_in = refs[10:15]
    total, mixed, sems, rim_sems = refs[15:]
    win = ext.shape[3]
    tile = ext.shape[2] - win
    place = Place(rows, cols)
    barrier = greet(place, NEXT)
    meet(place, barrier, NEXT)
    spills = spill_shifts(place, (side_spill, low_spill, corner_spill), got, mixed, sems)
    for shift in spills[:3]:
        shift.start()
    total[...] = spread[:, :2, :tile]
    pass_corner(spills, spread, side_spill, got[2], mixed)
    add_spills(spills, total, got)
    rims = rim_boxes(place, (side_out, low_out), (side_in, low_in, corner_in), win, rim_sems)
    for strip in range(2):
        share = 1.0 / (total[2, strip] + 4.0)
        for plane in range(2):
            fresh = obj[plane, :, strip * win : (strip + 1) * win] + total[plane, strip] * share
            if strip == 0:
                side_out[plane] = fresh.astype(jnp.bfloat16)
            low_out[plane, strip] = fresh[:win].astype(jnp.bfloat16)
            ext[plane, strip, :tile] = fresh
        inverse[strip] = share
        for rim in rims[:2] if strip == 0 else rims[2:3]:
            rim.start()
    finish_sends(spills)
    fill_rims(rims, ext, side_in, low_in, corner_in)
    finish_sends(rims)


def last_kernel(rows, cols, *refs):
    spread, side_spill, low_spill, corner_spill, gradient, narrow = refs[:6]
    total, whole = refs[6:8]
    got, mixed = refs[8:11], refs[11]
    part_in, peer_in, own, sems, part_sems, peer_sems, whole_sems = refs[12:]
    tile = total.shape[2]
    place = Place(rows, cols)
    barrier = pltpu.get_barrier_semaphore()
    col_peers = [place.at(0, step) for step in range(1, cols)]
    row_peers = [place.at(step, 0) for step in range(1, rows)]
    for peer in col_peers + row_peers:
        pl.semaphore_signal(barrier, inc=1, device_id=peer, device_id_type=MESH)
    pl.semaphore_wait(barrier, cols + rows - 2)
    height = whole.shape[0] // rows

    def piece(index):
        return pl.ds(pl.multiple_of(index * height, height), height)

    def send(source, target, pair, index, peer):
        copy = pltpu.make_async_remote_copy(
            src_ref=source,
            dst_ref=target,
            send_sem=pair.at[0, index],
            recv_sem=pair.at[1, index],
            device_id=peer,
            device_id_type=MESH,
        )
        copy.start()
        return copy

    parts = [
        send(narrow.at[piece(peer[0])], part_in.at[index], part_sems, index, peer)
        for index, peer in enumerate(row_peers)
    ]
    spills = spill_shifts(place, (side_spill, low_spill, corner_spill), got, mixed, sems)
    for shift in spills[:3]:
        shift.start()
    summed = gradient[piece(place.row)]
    for index, copy in enumerate(parts):
        copy.wait_recv()
        summed = summed + part_in[index].astype(jnp.float32)
    own[...] = summed.astype(jnp.bfloat16)
    peer_in[place.col] = summed.astype(jnp.bfloat16)
    peers = [
        send(own, peer_in.at[place.col], peer_sems, index, peer)
        for index, peer in enumerate(col_peers)
    ]
    pass_corner(spills, spread, side_spill, got[2], mixed)
    total[...] = spread[:, :2, :tile]
    for copy in peers:
        copy.wait_recv()
    summed = peer_in[0].astype(jnp.float32)
    for index in range(1, cols):
        summed = summed + peer_in[index].astype(jnp.float32)
    whole[piece(place.row)] = summed
    gathers = [
        send(whole.at[piece(place.row)], whole.at[piece(place.row)], whole_sems, index, peer)
        for index, peer in enumerate(row_peers)
    ]
    add_spills(spills, total, got)
    for copy in gathers:
        copy.wait_recv()
    for copy in parts + peers + gathers:
        copy.wait_send()
    finish_sends(spills)


def close_kernel(ext, total, inverse, whole, probe, refined, new_probe):
    win = ext.shape[3]
    tile = ext.shape[2] - win
    for strip in range(2):
        for plane in range(2):
            refined[plane, :, strip * win : (strip + 1) * win] = (
                ext[plane, strip, :tile] + total[plane, strip] * inverse[strip]
            )
    value = whole[...]
    power = jnp.sum(value * value, axis=(0, 1), keepdims=True) / (value.shape[0] // 2 * win)
    new_probe[...] = probe[...] + value * lax.rsqrt(power + 1e-06)


def remote_call(kernel, ident, out_shape, scratch, operands):
    vmem = pl.BlockSpec(memory_space=pltpu.VMEM)
    return pl.pallas_call(
        kernel,
        out_shape=out_shape,
        in_specs=[vmem] * len(operands),
        out_specs=[vmem] * len(out_shape),
        scratch_shapes=scratch,
        compiler_params=pltpu.CompilerParams(
            collective_id=ident, has_side_effects=True, vmem_limit_bytes=GRANT
        ),
    )(*operands)


def on_device(rows, cols, object_field, probe, amplitude, corners, live_count):
    slots = amplitude.shape[2]
    win = probe.shape[1]
    tile = object_field.shape[1]
    amp = amplitude.reshape(slots, win, win)
    corners = corners.reshape(2, slots)
    live = live_count.reshape(1)
    ahead, back = dft_tables(win)
    f32, b16 = jnp.float32, jnp.bfloat16
    sem = pltpu.SemaphoreType.DMA
    ext_shape = jax.ShapeDtypeStruct((2, tile // win + 1, tile + win, win), f32)

    def boxes(planes, count=3):
        return [pltpu.VMEM(shape, b16) for shape in spill_shapes(planes, tile, win)[:count]]

    (ext,) = remote_call(
        functools.partial(extend_kernel, rows, cols),
        0,
        [ext_shape],
        boxes(2, 2) + boxes(2) + [sem((2, 4))],
        [object_field],
    )
    spread, *spills = sweep(True, corners, live, ext, probe, amp, ahead, back)
    ext, inverse = remote_call(
        functools.partial(update_kernel, rows, cols),
        1,
        [ext_shape, jax.ShapeDtypeStruct((2, tile, win), f32)],
        boxes(3)
        + boxes(2, 2)
        + boxes(2)
        + [
            pltpu.VMEM((3, 2, tile, win), f32),
            pltpu.VMEM((3, win, win), b16),
            sem((2, 4)),
            sem((2, 4)),
        ],
        [spread, *spills, object_field],
    )
    spread, *spills, gradient, narrow = sweep(False, corners, live, ext, probe, amp, ahead, back)
    flat = (2 * win, win)
    height = 2 * win // rows
    total, whole = remote_call(
        functools.partial(last_kernel, rows, cols),
        2,
        [jax.ShapeDtypeStruct((2, 2, tile, win), f32), jax.ShapeDtypeStruct(flat, f32)],
        boxes(2)
        + [
            pltpu.VMEM((2, win, win), b16),
            pltpu.VMEM((rows - 1, height, win), b16),
            pltpu.VMEM((cols, height, win), b16),
            pltpu.VMEM((height, win), b16),
            sem((2, 4)),
            sem((2, rows - 1)),
            sem((2, cols - 1)),
            sem((2, rows - 1)),
        ],
        [spread, *spills, gradient.reshape(flat), narrow.reshape(flat)],
    )
    vmem = pl.BlockSpec(memory_space=pltpu.VMEM)
    refined, new_probe = pl.pallas_call(
        close_kernel,
        out_shape=[jax.ShapeDtypeStruct(object_field.shape, f32), jax.ShapeDtypeStruct(flat, f32)],
        in_specs=[vmem] * 5,
        out_specs=[vmem] * 2,
        compiler_params=pltpu.CompilerParams(vmem_limit_bytes=GRANT),
        name="close",
    )(ext, total, inverse, whole, probe.reshape(flat))
    return (refined, new_probe.reshape(probe.shape))


def solution(mesh):
    in_specs = (
        P(None, "row", "col"),
        P(),
        P("row", "col", None, None, None),
        P(None, "row", "col", None),
        P("row", "col"),
    )
    out_specs = (P(None, "row", "col"), P())
    return jax.shard_map(
        functools.partial(on_device, mesh.shape["row"], mesh.shape["col"]), mesh=mesh, in_specs=in_specs, out_specs=out_specs, check_vma=False
    )
```

```python
import functools
import math

import jax
import jax.numpy as jnp
import numpy as np
from jax import lax
from jax.experimental import pallas as pl
from jax.experimental.pallas import tpu as pltpu
from jax.sharding import PartitionSpec as P

GROUP = 16
GRANT = 12 << 20


def dft_tables(window):
    indices = np.arange(window, dtype=np.int32)
    phase_index = indices[:, None] * indices[None, :] % window
    angles = phase_index.astype(np.float32) * np.float32(2.0 * math.pi / window)
    norming = np.float32(1.0 / math.sqrt(window))
    cosines = np.cos(angles) * norming
    sines = np.sin(angles) * norming
    forward = np.block([[cosines, -sines], [sines, cosines]]).astype(np.float32)
    return (jnp.asarray(forward, jnp.bfloat16), jnp.asarray(forward.T.copy(), jnp.bfloat16))


def dot(left, right):
    return jnp.dot(left, right, preferred_element_type=jnp.float32)


def sweep_kernel(with_light, corners, live, ext, probe, amp, ahead, back, deposit, *rest):
    side_out, low_out, corner_out = rest[:3]
    if with_light:
        waves_buf = rest[3]
    else:
        gradient, narrow, waves_buf, patch_buf = rest[3:]
        gradient[...] = jnp.zeros_like(gradient)
    slots, win = amp.shape[0], amp.shape[1]
    deposit[...] = jnp.zeros_like(deposit)
    lane = lax.broadcasted_iota(jnp.int32, (win, win), 1)
    used = live[0]

    def spot(slot):
        row, col = corners[0, slot], corners[1, slot]
        base = col // win
        return row, base, col - base * win

    def add_at(plane, row, base, shift, value):
        turned = pltpu.roll(value, shift, 1)
        left = jnp.where(lane >= shift, turned, 0.0)
        right = jnp.where(lane >= shift, 0.0, turned)
        for offset, part in ((0, left), (1, right)):
            at = (plane, base + offset, pl.ds(row, win))
            deposit[at] = deposit[at] + part

    @pl.loop(0, (used + GROUP - 1) // GROUP)
    def _(turn):
        first = turn * GROUP
        pr, pi = probe[0], probe[1]
        for member in range(GROUP):
            row, base, shift = spot(first + member)
            parts = []
            for plane in range(2):
                left = ext[plane, base, pl.ds(row, win)]
                right = ext[plane, base + 1, pl.ds(row, win)]
                mixed = jnp.where(lane >= shift, left, right)
                parts.append(pltpu.roll(mixed, lax.rem(win - shift, win), 1))
            re, im = parts
            if not with_light:
                patch_buf[member, 0] = re
                patch_buf[member, 1] = im
            rows = pl.ds(member * win, win)
            waves_buf[rows, :win] = (pr * re - pi * im).astype(jnp.bfloat16)
            waves_buf[rows, win:] = (pr * im + pi * re).astype(jnp.bfloat16)
        half = dot(waves_buf[...], ahead[...]).astype(jnp.bfloat16)

        def upright(value):
            columns = []
            for member in range(GROUP):
                block = value[member * win : (member + 1) * win]
                columns.append(jnp.concatenate([block[:, :win], block[:, win:]], 0))
            return jnp.concatenate(columns, 1)

        spectrum = dot(back[...], upright(half))
        projected = []
        for member in range(GROUP):
            re = spectrum[:win, member * win : (member + 1) * win]
            im = spectrum[win:, member * win : (member + 1) * win]
            scale = amp[first + member].astype(jnp.float32) * lax.rsqrt(
                jnp.maximum(re * re + im * im, 0.25)
            )
            projected.append(
                jnp.concatenate(
                    [(re * scale).astype(jnp.bfloat16), (im * scale).astype(jnp.bfloat16)], 1
                )
            )
        half_back = dot(jnp.concatenate(projected, 0), back[...]).astype(jnp.bfloat16)
        returned = dot(ahead[...], upright(half_back))
        for member in range(GROUP):
            slot = first + member
            weight = jnp.where(slot < used, 1.0, 0.0)
            row, base, shift = spot(slot)
            rows = pl.ds(member * win, win)
            columns = slice(member * win, (member + 1) * win)
            re = (returned[:win, columns] - waves_buf[rows, :win].astype(jnp.float32)) * weight
            im = (returned[win:, columns] - waves_buf[rows, win:].astype(jnp.float32)) * weight
            add_at(0, row, base, shift, pr * re + pi * im)
            add_at(1, row, base, shift, pr * im - pi * re)
            if with_light:
                add_at(2, row, base, shift, (pr * pr + pi * pi) * weight)
            else:
                ore, oim = patch_buf[member, 0], patch_buf[member, 1]
                gradient[0] += ore * re + oim * im
                gradient[1] += ore * im - oim * re

    tile = deposit.shape[2] - win
    side_out[...] = deposit[:, 2, :tile].astype(jnp.bfloat16)
    low_out[...] = deposit[:, :2, tile:].astype(jnp.bfloat16)
    corner_out[...] = deposit[:, 2, tile:].astype(jnp.bfloat16)
    if not with_light:
        narrow[...] = gradient[...].astype(jnp.bfloat16)


def spill_shapes(planes, tile, win):
    return [(planes, tile, win), (planes, 2, win, win), (planes, win, win)]


def sweep(with_light, corners, live, ext, probe, amp, ahead, back):
    slots, win = amp.shape[0], amp.shape[1]
    strips, side = ext.shape[1:3]
    vmem = pl.BlockSpec(memory_space=pltpu.VMEM)
    smem = pl.BlockSpec(memory_space=pltpu.SMEM)
    planes = 3 if with_light else 2
    out_shape = [jax.ShapeDtypeStruct((planes, strips, side, win), jnp.float32)]
    for shape in spill_shapes(planes, side - win, win):
        out_shape.append(jax.ShapeDtypeStruct(shape, jnp.bfloat16))
    scratch = [pltpu.VMEM((GROUP * win, 2 * win), jnp.bfloat16)]
    if not with_light:
        out_shape.append(jax.ShapeDtypeStruct((2, win, win), jnp.float32))
        out_shape.append(jax.ShapeDtypeStruct((2, win, win), jnp.bfloat16))
        scratch.append(pltpu.VMEM((GROUP, 2, win, win), jnp.float32))
    return pl.pallas_call(
        functools.partial(sweep_kernel, with_light),
        out_shape=out_shape,
        in_specs=[smem, smem] + [vmem] * 5,
        out_specs=[vmem] * len(out_shape),
        scratch_shapes=scratch,
        compiler_params=pltpu.CompilerParams(vmem_limit_bytes=GRANT),
        name="first_sweep" if with_light else "second_sweep",
    )(corners, live, ext, probe, amp, ahead, back)


MESH = pl.DeviceIdType.MESH


class Place:
    def __init__(self, rows, cols):
        self.row, self.col = lax.axis_index("row"), lax.axis_index("col")
        self.rows, self.cols = rows, cols

    def at(self, down, right):
        return (
            lax.rem(self.row + down + self.rows, self.rows),
            lax.rem(self.col + right + self.cols, self.cols),
        )

    def inside(self, down, right):
        checks = []
        if down:
            checks.append(self.row < self.rows - 1 if down > 0 else self.row > 0)
        if right:
            checks.append(self.col < self.cols - 1 if right > 0 else self.col > 0)
        return checks[0] if len(checks) == 1 else jnp.logical_and(*checks)


def greet(place, steps):
    barrier = pltpu.get_barrier_semaphore()
    for step in steps:

        @pl.when(place.inside(*step))
        def _():
            pl.semaphore_signal(barrier, inc=1, device_id=place.at(*step), device_id_type=MESH)

    return barrier


def meet(place, barrier, steps, others=0):
    for step in steps:
        others = others + jnp.where(place.inside(*step), 1, 0)
    pl.semaphore_wait(barrier, others)


NEXT = ((0, -1), (-1, 0), (0, 1), (1, 0))


class Shift:
    def __init__(self, place, step, source, target, sems, index):
        self.copy = pltpu.make_async_remote_copy(
            src_ref=source,
            dst_ref=target,
            send_sem=sems.at[0, index],
            recv_sem=sems.at[1, index],
            device_id=place.at(*step),
            device_id_type=MESH,
        )
        self.sends = place.inside(*step)
        self.receives = place.inside(-step[0], -step[1])

    def start(self):
        pl.when(self.sends)(self.copy.start)

    def wait_send(self):
        pl.when(self.sends)(self.copy.wait_send)


def spill_shifts(place, spills, got, mixed, sems):
    side, low, corner = spills
    side_got, low_got, corner_got = got
    win = corner.shape[1]
    top, bottom = pl.ds(0, win), pl.ds(win, side.shape[1] - win)
    below = Shift(place, (1, 0), corner, corner_got, sems, 0)
    below.sends = place.inside(1, 1)
    below.receives = place.inside(-1, 1)
    return [
        below,
        Shift(place, (0, 1), side.at[:, bottom], side_got.at[:, bottom], sems, 1),
        Shift(place, (1, 0), low, low_got, sems, 2),
        Shift(place, (0, 1), mixed, side_got.at[:, top], sems, 3),
    ]


def pass_corner(shifts, spread, side, corner_got, mixed):
    win = corner_got.shape[1]
    below = shifts[0]

    @pl.when(below.receives)
    def _():
        below.copy.wait_recv()
        mixed[...] = (spread[:, 2, :win] + corner_got[...].astype(jnp.float32)).astype(jnp.bfloat16)

    @pl.when(jnp.logical_not(below.receives))
    def _():
        mixed[...] = side[:, :win]

    shifts[3].start()


def finish_sends(shifts):
    for shift in shifts:
        shift.wait_send()


def fill_rims(shifts, ext, side_in, low_in, corner_in):
    win = ext.shape[3]
    tile = ext.shape[2] - win
    top, bottom, low, onward = shifts

    @pl.when(top.receives)
    def _():
        top.copy.wait_recv()

    onward.start()

    @pl.when(low.receives)
    def _():
        low.copy.wait_recv()
        ext[:, :2, tile:] = low_in[...].astype(jnp.float32)

    @pl.when(bottom.receives)
    def _():
        bottom.copy.wait_recv()
        ext[:, 2, :tile] = side_in[...].astype(jnp.float32)

    @pl.when(onward.receives)
    def _():
        onward.copy.wait_recv()
        ext[:, 2, tile:] = corner_in[...].astype(jnp.float32)


def add_spills(shifts, total, got):
    side_got, low_got, corner_got = got
    win = total.shape[3]
    below, bottom, low, top = shifts

    @pl.when(low.receives)
    def _():
        low.copy.wait_recv()
        total[:, :, :win] += low_got[...].astype(jnp.float32)

    @pl.when(bottom.receives)
    def _():
        bottom.copy.wait_recv()
        total[:, 0, win:] += side_got[:, win:].astype(jnp.float32)

    @pl.when(top.receives)
    def _():
        top.copy.wait_recv()
        total[:, 0, :win] += side_got[:, :win].astype(jnp.float32)


def rim_boxes(place, outs, ins, win, sems):
    side_out, low_out = outs
    side_in, low_in, corner_in = ins
    top, bottom = pl.ds(0, win), pl.ds(win, side_in.shape[1] - win)
    left = (0, -1)
    onward = Shift(place, (-1, 0), side_in.at[:, top], corner_in, sems, 3)
    onward.sends = place.inside(-1, 1)
    onward.receives = place.inside(1, 1)
    return [
        Shift(place, left, side_out.at[:, top], side_in.at[:, top], sems, 0),
        Shift(place, left, side_out.at[:, bottom], side_in.at[:, bottom], sems, 1),
        Shift(place, (-1, 0), low_out, low_in, sems, 2),
        onward,
    ]


def extend_kernel(rows, cols, obj, ext, side_out, low_out, side_in, low_in, corner_in, sems):
    win = ext.shape[3]
    tile = ext.shape[2] - win
    place = Place(rows, cols)
    barrier = greet(place, NEXT)
    side_out[...] = obj[:, :, :win].astype(jnp.bfloat16)
    for strip in range(2):
        low_out[:, strip] = obj[:, :win, strip * win : (strip + 1) * win].astype(jnp.bfloat16)
    meet(place, barrier, NEXT)
    shifts = rim_boxes(place, (side_out, low_out), (side_in, low_in, corner_in), win, sems)
    for shift in shifts[:3]:
        shift.start()
    for strip in range(2):
        ext[:, strip, :tile] = obj[:, :, strip * win : (strip + 1) * win]
    fill_rims(shifts, ext, side_in, low_in, corner_in)
    finish_sends(shifts)


def update_kernel(rows, cols, *refs):
    spread, side_spill, low_spill, corner_spill, obj, ext, inverse = refs[:7]
    got = refs[7:10]
    side_out, low_out, side_in, low_in, corner_in = refs[10:15]
    total, mixed, sems, rim_sems = refs[15:]
    win = ext.shape[3]
    tile = ext.shape[2] - win
    place = Place(rows, cols)
    barrier = greet(place, NEXT)
    meet(place, barrier, NEXT)
    spills = spill_shifts(place, (side_spill, low_spill, corner_spill), got, mixed, sems)
    for shift in spills[:3]:
        shift.start()
    total[...] = spread[:, :2, :tile]
    pass_corner(spills, spread, side_spill, got[2], mixed)
    add_spills(spills, total, got)
    rims = rim_boxes(place, (side_out, low_out), (side_in, low_in, corner_in), win, rim_sems)
    for strip in range(2):
        share = 1.0 / (total[2, strip] + 4.0)
        for plane in range(2):
            fresh = obj[plane, :, strip * win : (strip + 1) * win] + total[plane, strip] * share
            if strip == 0:
                side_out[plane] = fresh.astype(jnp.bfloat16)
            low_out[plane, strip] = fresh[:win].astype(jnp.bfloat16)
            ext[plane, strip, :tile] = fresh
        inverse[strip] = share
        for rim in rims[:2] if strip == 0 else rims[2:3]:
            rim.start()
    finish_sends(spills)
    fill_rims(rims, ext, side_in, low_in, corner_in)
    finish_sends(rims)


def last_kernel(rows, cols, *refs):
    spread, side_spill, low_spill, corner_spill, gradient, narrow = refs[:6]
    total, whole = refs[6:8]
    got, mixed = refs[8:11], refs[11]
    part_in, peer_in, own, sems, part_sems, peer_sems, whole_sems = refs[12:]
    tile = total.shape[2]
    place = Place(rows, cols)
    barrier = pltpu.get_barrier_semaphore()
    col_peers = [place.at(0, step) for step in range(1, cols)]
    row_peers = [place.at(step, 0) for step in range(1, rows)]
    for peer in col_peers + row_peers:
        pl.semaphore_signal(barrier, inc=1, device_id=peer, device_id_type=MESH)
    pl.semaphore_wait(barrier, cols + rows - 2)
    height = whole.shape[0] // rows

    def piece(index):
        return pl.ds(pl.multiple_of(index * height, height), height)

    def send(source, target, pair, index, peer):
        copy = pltpu.make_async_remote_copy(
            src_ref=source,
            dst_ref=target,
            send_sem=pair.at[0, index],
            recv_sem=pair.at[1, index],
            device_id=peer,
            device_id_type=MESH,
        )
        copy.start()
        return copy

    parts = [
        send(narrow.at[piece(peer[0])], part_in.at[index], part_sems, index, peer)
        for index, peer in enumerate(row_peers)
    ]
    spills = spill_shifts(place, (side_spill, low_spill, corner_spill), got, mixed, sems)
    for shift in spills[:3]:
        shift.start()
    summed = gradient[piece(place.row)]
    for index, copy in enumerate(parts):
        copy.wait_recv()
        summed = summed + part_in[index].astype(jnp.float32)
    own[...] = summed.astype(jnp.bfloat16)
    peer_in[place.col] = summed.astype(jnp.bfloat16)
    peers = [
        send(own, peer_in.at[place.col], peer_sems, index, peer)
        for index, peer in enumerate(col_peers)
    ]
    pass_corner(spills, spread, side_spill, got[2], mixed)
    total[...] = spread[:, :2, :tile]
    for copy in peers:
        copy.wait_recv()
    summed = peer_in[0].astype(jnp.float32)
    for index in range(1, cols):
        summed = summed + peer_in[index].astype(jnp.float32)
    whole[piece(place.row)] = summed
    gathers = [
        send(whole.at[piece(place.row)], whole.at[piece(place.row)], whole_sems, index, peer)
        for index, peer in enumerate(row_peers)
    ]
    add_spills(spills, total, got)
    for copy in gathers:
        copy.wait_recv()
    for copy in parts + peers + gathers:
        copy.wait_send()
    finish_sends(spills)


def close_kernel(ext, total, inverse, whole, probe, refined, new_probe):
    win = ext.shape[3]
    tile = ext.shape[2] - win
    for strip in range(2):
        for plane in range(2):
            refined[plane, :, strip * win : (strip + 1) * win] = (
                ext[plane, strip, :tile] + total[plane, strip] * inverse[strip]
            )
    value = whole[...]
    power = jnp.sum(value * value, axis=(0, 1), keepdims=True) / (value.shape[0] // 2 * win)
    new_probe[...] = probe[...] + value * lax.rsqrt(power + 1e-06)


def remote_call(kernel, ident, out_shape, scratch, operands):
    vmem = pl.BlockSpec(memory_space=pltpu.VMEM)
    return pl.pallas_call(
        kernel,
        out_shape=out_shape,
        in_specs=[vmem] * len(operands),
        out_specs=[vmem] * len(out_shape),
        scratch_shapes=scratch,
        compiler_params=pltpu.CompilerParams(
            collective_id=ident, has_side_effects=True, vmem_limit_bytes=GRANT
        ),
    )(*operands)


def on_device(rows, cols, object_field, probe, amplitude, corners, live_count):
    slots = amplitude.shape[2]
    win = probe.shape[1]
    tile = object_field.shape[1]
    amp = amplitude.reshape(slots, win, win)
    corners = corners.reshape(2, slots)
    live = live_count.reshape(1)
    ahead, back = dft_tables(win)
    f32, b16 = jnp.float32, jnp.bfloat16
    sem = pltpu.SemaphoreType.DMA
    ext_shape = jax.ShapeDtypeStruct((2, tile // win + 1, tile + win, win), f32)

    def boxes(planes, count=3):
        return [pltpu.VMEM(shape, b16) for shape in spill_shapes(planes, tile, win)[:count]]

    (ext,) = remote_call(
        functools.partial(extend_kernel, rows, cols),
        0,
        [ext_shape],
        boxes(2, 2) + boxes(2) + [sem((2, 4))],
        [object_field],
    )
    spread, *spills = sweep(True, corners, live, ext, probe, amp, ahead, back)
    ext, inverse = remote_call(
        functools.partial(update_kernel, rows, cols),
        1,
        [ext_shape, jax.ShapeDtypeStruct((2, tile, win), f32)],
        boxes(3)
        + boxes(2, 2)
        + boxes(2)
        + [
            pltpu.VMEM((3, 2, tile, win), f32),
            pltpu.VMEM((3, win, win), b16),
            sem((2, 4)),
            sem((2, 4)),
        ],
        [spread, *spills, object_field],
    )
    spread, *spills, gradient, narrow = sweep(False, corners, live, ext, probe, amp, ahead, back)
    flat = (2 * win, win)
    height = 2 * win // rows
    total, whole = remote_call(
        functools.partial(last_kernel, rows, cols),
        2,
        [jax.ShapeDtypeStruct((2, 2, tile, win), f32), jax.ShapeDtypeStruct(flat, f32)],
        boxes(2)
        + [
            pltpu.VMEM((2, win, win), b16),
            pltpu.VMEM((rows - 1, height, win), b16),
            pltpu.VMEM((cols, height, win), b16),
            pltpu.VMEM((height, win), b16),
            sem((2, 4)),
            sem((2, rows - 1)),
            sem((2, cols - 1)),
            sem((2, rows - 1)),
        ],
        [spread, *spills, gradient.reshape(flat), narrow.reshape(flat)],
    )
    vmem = pl.BlockSpec(memory_space=pltpu.VMEM)
    refined, new_probe = pl.pallas_call(
        close_kernel,
        out_shape=[jax.ShapeDtypeStruct(object_field.shape, f32), jax.ShapeDtypeStruct(flat, f32)],
        in_specs=[vmem] * 5,
        out_specs=[vmem] * 2,
        compiler_params=pltpu.CompilerParams(vmem_limit_bytes=GRANT),
        name="close",
    )(ext, total, inverse, whole, probe.reshape(flat))
    return (refined, new_probe.reshape(probe.shape))


def solution(mesh):
    in_specs = (
        P(None, "row", "col"),
        P(),
        P("row", "col", None, None, None),
        P(None, "row", "col", None),
        P("row", "col"),
    )
    out_specs = (P(None, "row", "col"), P())
    return jax.shard_map(
        functools.partial(on_device, mesh.shape["row"], mesh.shape["col"]), mesh=mesh, in_specs=in_specs, out_specs=out_specs, check_vma=False
    )
```
